32 devices in a mesh: dp: 2 (over y), ctx: 2 (over core), expert: 8 (over z, x).
Axes of the slice: x: 2, y: 2, z: 4, core: 2. Of those that a mesh axis runs over, the one named last changes fastest.
Arguments:
- hidden_in: bfloat16 [4, 1024, 2048], P('dp', ('ctx', 'expert')), may hold values from -9 to 9
- out_grad: bfloat16 [4, 1024, 2048], P('dp', ('ctx', 'expert')), may hold values from -6 to 6
- routes: int32 [4, 1024, 6], P('dp', ('ctx', 'expert')), may hold values from 0 to 15, all different within a row; in each aligned block of 64 rows (0 to 63, 64 to 127, ..., all dimensions but the last counted through in order) at most 32 rows name the same one
- block_order: int32 [4, 4], P('dp'), may hold values from 0 to 3, as said below
- norm_attn: float32 [2048], replicated, may hold values from 0.25 to 1.75
- w_query: bfloat16 [2048, 3072], P(None, 'expert'), may hold values from -0.088388348 to 0.088388348
- w_kv_down: bfloat16 [2048, 576], P('expert'), may hold values from -0.088388348 to 0.088388348
- norm_latent: float32 [512], replicated, may hold values from 0.25 to 1.75
- w_key_up: bfloat16 [512, 2048], P(None, 'expert'), may hold values from -0.25 to 0.25
- w_value_up: bfloat16 [512, 2048], P(None, 'expert'), may hold values from -0.25 to 0.25
- w_out: bfloat16 [2048, 2048], P('expert'), may hold values from -3 to 3
- norm_ffn: float32 [2048], replicated, may hold values from 0.25 to 1.75
- w_router: bfloat16 [2048, 16], replicated, may hold values from -0.25 to 0.25
- shared_gate: bfloat16 [2048, 2816], P(None, 'expert'), may hold values from -0.125 to 0.125
- shared_up: bfloat16 [2048, 2816], P(None, 'expert'), may hold values from -0.125 to 0.125
- shared_down: bfloat16 [2816, 2048], P('expert'), may hold values from -0.109375 to 0.109375
- expert_gate: bfloat16 [16, 2048, 1408], P(('dp', 'expert')), may hold values from -0.125 to 0.125
- expert_up: bfloat16 [16, 2048, 1408], P(('dp', 'expert')), may hold values from -0.125 to 0.125
- expert_down: bfloat16 [16, 1408, 2048], P(('dp', 'expert')), may hold values from -0.15625 to 0.15625
Outputs:
- out_hidden: bfloat16 [4, 1024, 2048], P('dp', ('ctx', 'expert'))
- in_grad: bfloat16 [4, 1024, 2048], P('dp', ('ctx', 'expert'))
- grad_norm_attn: float32 [2048], P('expert')
- grad_query: float32 [2048, 3072], P(None, 'expert')
- grad_kv_down: float32 [2048, 576], P('expert')
- grad_norm_latent: float32 [512], P('expert')
- grad_key_up: float32 [512, 2048], P(None, 'expert')
- grad_value_up: float32 [512, 2048], P(None, 'expert')
- grad_out_proj: float32 [2048, 2048], P('expert')
- grad_norm_ffn: float32 [2048], P('expert')
- grad_router: float32 [2048, 16], P('expert')
- grad_shared_gate: float32 [2048, 2816], P(None, 'expert')
- grad_shared_up: float32 [2048, 2816], P(None, 'expert')
- grad_shared_down: float32 [2816, 2048], P('expert')
- grad_expert_gate: float32 [16, 2048, 1408], P(('dp', 'expert'), 'ctx')
- grad_expert_up: float32 [16, 2048, 1408], P(('dp', 'expert'), 'ctx')
- grad_expert_down: float32 [16, 1408, 2048], P(('dp', 'expert'), 'ctx')
The draws below stay inside these ranges and needn't reach their ends.
Inputs may be any that keep to these rules, and one draw needn't show every extreme that they name: `routes`: each row names 6 different experts. In the rows of one sequence on one device (64 aligned rows) no expert is named by more than 32 rows, a bound that some block reaches. `block_order`: each sequence's row is a permutation of 0 to 3 in which entries 2 c and 2 c + 1 sum to 3.
All inputs are finite; a program needn't handle non-finite values.
Results may differ from the reference program's by a relative error of at most 0.035.
Values may be sent and summed in bfloat16 or wider, within the bound.
No kernel may reach another device: no remote copies, remote signals or barrier semaphores. Data moves between devices by JAX's collectives and lax.ppermute only.
A program may use at most 320 MiB of HBM per device.

```python
import math
import jax
import jax.numpy as jnp
import numpy as np
from jax import lax

D = 2048
HEADS = 16
NOPE = 128
ROPE = 64
VDIM = 128
LATENT = 512
F_EXP = 1408
F_SHARED = 2816
TOP = 6
PIECE = 64
LENGTH = 1024
SEQS = 4
EXPERTS = 16
MOST = 32
HALVES = 4
N_CTX = 2


def draw_block_order(key, part):
    pair_key, flip_key = jax.random.split(jax.random.fold_in(key, 17))
    pair_ids = jax.vmap(lambda row_key: jax.random.permutation(row_key, HALVES // 2))(jax.random.split(pair_key, SEQS))
    flip_bits = jax.random.randint(flip_key, (SEQS, HALVES // 2), 0, 2)
    leading = jnp.where(flip_bits == 1, HALVES - 1 - pair_ids, pair_ids)
    trailing = HALVES - 1 - leading
    return jnp.stack([leading, trailing], axis=-1).reshape(SEQS, HALVES).astype(jnp.int32)


def rope_block(key):
    block_key, head_key = jax.random.split(jax.random.fold_in(key, 101))
    block = jnp.clip(jax.random.normal(block_key, (D, ROPE), jnp.float32), -3.0, 3.0) * D ** (-0.5)
    chosen_head = jax.random.randint(head_key, (), 0, HEADS)
    return (block, chosen_head)


def draw_w_query(key, part):
    block, chosen_head = rope_block(key)
    width = HEADS * (NOPE + ROPE)
    base = jnp.clip(jax.random.normal(jax.random.fold_in(key, 102), (D, width), jnp.float32), -4.0, 4.0) * D ** (-0.5)
    columns = jnp.arange(width, dtype=jnp.int32)
    inside = columns % (NOPE + ROPE)
    rope_column = jnp.clip(inside - NOPE, 0, ROPE - 1)
    copied = jnp.take(block, rope_column, axis=1)
    selected = (columns // (NOPE + ROPE) == chosen_head) & (inside >= NOPE)
    return jnp.where(selected[None, :], copied, base).astype(jnp.bfloat16)


def draw_w_kv_down(key, part):
    block, chosen_head = rope_block(key)
    base = jnp.clip(jax.random.normal(jax.random.fold_in(key, 103), (D, LATENT), jnp.float32), -4.0, 4.0) * D ** (-0.5)
    factor = jax.random.uniform(jax.random.fold_in(key, 104), (D, ROPE), jnp.float32, 0.85, 1.15)
    return jnp.concatenate([base, block * factor], axis=1).astype(jnp.bfloat16)


def draw_hidden_in(key, part):
    block, chosen_head = rope_block(key)
    noise_key, sign_key, row_key = jax.random.split(jax.random.fold_in(key, 105), 3)
    base = jnp.clip(jax.random.normal(noise_key, (SEQS, LENGTH, D), jnp.float32), -6.0, 6.0)
    strengths = [120.0, 170.0, 240.0, 330.0]
    band = (jnp.arange(ROPE, dtype=jnp.int32) % (ROPE // 2) >= ROPE // 4).astype(jnp.float32)
    signs = jnp.where(jax.random.bernoulli(sign_key, 0.5, (SEQS, 4, ROPE)), 1.0, -1.0) * band * (ROPE // 2) ** (-0.5)
    directions = jnp.sum(signs[:, :, None, :] * block[None, None, :, :], axis=-1)
    pair_rows = 2 * jax.random.randint(row_key, (SEQS, 4), 0, LENGTH // 2)
    row_ids = jnp.arange(LENGTH, dtype=jnp.int32)
    unit = (NOPE + ROPE) ** 0.5 * D ** (-0.5)
    planted = jnp.zeros((SEQS, LENGTH, D), jnp.float32)
    marked = jnp.zeros((SEQS, LENGTH), jnp.bool_)
    for pair in range(4):
        first = row_ids[None, :] == pair_rows[:, pair][:, None]
        second = row_ids[None, :] == pair_rows[:, pair][:, None] + 1
        amount = strengths[pair] * unit
        amplitude = jnp.where(first, amount, jnp.where(second, amount + 2.0 * unit, 0.0))
        planted = planted + amplitude[:, :, None] * directions[:, pair][:, None, :]
        marked = marked | first | second
    mixed = jnp.where(marked[:, :, None], planted + 0.15 * base, base)
    return jnp.clip(mixed, -9.0, 9.0).astype(jnp.bfloat16)


def levels(own_key, dims, pieces, smallest, top_value):
    gain, own = 1.0, jax.random.fold_in(own_key, 6)
    for axis_at, parts in pieces:
        draws = jnp.exp(jax.random.uniform(jax.random.fold_in(own, axis_at), (parts,), jnp.float32, smallest / len(pieces), top_value / len(pieces)))
        gain = gain * jnp.repeat(draws, dims[axis_at] // parts).reshape([-1 if axis == axis_at else 1 for axis in range(len(dims))])
    return gain


def deal_out(rng, own, number, rows, count, top, limit, lean):
    order = jax.random.permutation(rng, count)
    heavy_load, common = shares(count, rows * top, limit, lean, True), shares(count, rows * top, limit, lean, False)
    places = jnp.arange(count)

    def named(lengths, rotation):
        used = int((lengths > 0).sum())
        fixed = max(1, used // 4)
        shifted = fixed + (places - fixed + rotation * (used - fixed)) % max(1, count - fixed)
        return jnp.zeros((count,), jnp.int32).at[order[jnp.where(places < fixed, places, shifted)]].set(jnp.asarray(lengths, jnp.int32))

    lengths = jnp.where(number % 4 == 0, named(heavy_load, number // 4), named(common, number - number // 4 - 1))
    mixed = jax.random.permutation(jax.random.fold_in(own, 3), count)
    source_of, receiver = mixed[0:count // 2 * 2:2], mixed[1:count // 2 * 2:2]
    margin = jnp.minimum(lengths[source_of] - 1, limit - lengths[receiver]) // 2
    margin = jnp.where((source_of == order[0]) | (receiver == order[0]) | (lengths[receiver] == 0), 0, jnp.maximum(margin, 0))
    shifted = jax.random.randint(jax.random.fold_in(own, 4), (count // 2,), 0, 1 << 20) % (margin + 1)
    lengths = lengths.at[source_of].add(-shifted).at[receiver].add(shifted)
    items = jnp.searchsorted(jnp.cumsum(lengths), jnp.arange(rows * top), side="right").astype(jnp.int32)
    grid = items.reshape(top, rows).T
    grid = grid[jax.random.permutation(jax.random.fold_in(own, 1), rows)]
    rotation = jax.random.randint(jax.random.fold_in(own, 2), (rows, 1), 0, top)
    return jnp.take_along_axis(grid, (jnp.arange(top)[None, :] + rotation) % top, axis=1)


def shares(count, total, most, lean, full):
    loads = [(1 << 20) // math.isqrt(grade ** lean) + 1 for grade in range(1, count + 1)]
    largest = most if full else min(most, max(-(-total // count), total * loads[0] // sum(loads)))
    least = 1 if total - largest >= count - 1 else 0
    holding, spare = [largest] + [least] * (count - 1), total - largest - least * (count - 1)
    while spare > 0:
        movable = [i for i in range(1, count) if holding[i] < largest] or [i for i in range(1, count) if holding[i] < most]
        pool, remaining = sum([loads[i] for i in movable]), spare
        for i in movable:
            extra = min(most - holding[i], max(1, remaining * loads[i] // pool), spare)
            holding[i] = holding[i] + extra
            spare = spare - extra
    return np.array(holding)


def gaussian(stream_key, shape, spread, bound, cuts=(), kind=jnp.bfloat16):
    drawn = jax.random.normal(stream_key, shape, jnp.float32) * spread
    if len(cuts) > 0:
        drawn = levels(stream_key, shape, cuts, -0.22, 0.18) * drawn
    return jnp.clip(drawn, min=-bound, max=bound).astype(kind)


def setup_inputs(seed: int = 0) -> dict:
    arg_keys = jax.random.split(jax.random.key(seed), 20)
    hidden_in = draw_hidden_in(jax.random.fold_in(arg_keys[19], 71), 0)
    out_grad = gaussian(arg_keys[1], (SEQS, LENGTH, D), 1.0, 6.0, ((0, 2), (1, 16)))
    routes_keys = jax.random.split(jax.random.fold_in(arg_keys[2], 1), SEQS * LENGTH // PIECE)
    routes_turns = jax.random.permutation(jax.random.fold_in(arg_keys[2], 3), SEQS * LENGTH // PIECE)
    routes = jax.vmap(lambda own, number: deal_out(jax.random.fold_in(arg_keys[2], 2), own, number, PIECE, EXPERTS, TOP, MOST, 2))(routes_keys, routes_turns).reshape((SEQS, LENGTH, TOP))
    block_order = draw_block_order(jax.random.fold_in(arg_keys[19], 71), 0)
    norm_attn = jnp.clip(1.0 + 0.15 * jax.random.normal(arg_keys[4], (D,), jnp.float32), 0.25, 1.75)
    w_query = draw_w_query(jax.random.fold_in(arg_keys[19], 71), 0)
    w_kv_down = draw_w_kv_down(jax.random.fold_in(arg_keys[19], 71), 0)
    norm_latent = jnp.clip(1.0 + 0.15 * jax.random.normal(arg_keys[7], (LATENT,), jnp.float32), 0.25, 1.75)
    w_key_up = gaussian(arg_keys[8], (LATENT, HEADS * NOPE), LATENT ** -0.5, 0.25, ((1, 8),))
    w_value_up = gaussian(arg_keys[9], (LATENT, HEADS * VDIM), LATENT ** -0.5, 0.25, ((1, 8),))
    w_out = gaussian(arg_keys[10], (HEADS * VDIM, D), (max(1, 2 * HEADS * VDIM // LENGTH)) ** -0.5, 3.0, ((0, 8),))
    norm_ffn = jnp.clip(1.0 + 0.15 * jax.random.normal(arg_keys[11], (D,), jnp.float32), 0.25, 1.75)
    w_router = gaussian(arg_keys[12], (D, EXPERTS), (D // 4) ** -0.5, 0.25)
    shared_gate = gaussian(arg_keys[13], (D, F_SHARED), D ** -0.5, 0.125, ((1, 8),))
    shared_up = gaussian(arg_keys[14], (D, F_SHARED), D ** -0.5, 0.125, ((1, 8),))
    shared_down = gaussian(arg_keys[15], (F_SHARED, D), F_SHARED ** -0.5, 0.109375, ((0, 8),))
    expert_gate = gaussian(arg_keys[16], (EXPERTS, D, F_EXP), D ** -0.5, 0.125, ((0, 16),))
    expert_up = gaussian(arg_keys[17], (EXPERTS, D, F_EXP), D ** -0.5, 0.125, ((0, 16),))
    expert_down = gaussian(arg_keys[18], (EXPERTS, F_EXP, D), F_EXP ** -0.5, 0.15625, ((0, 16),))
    return {"hidden_in": hidden_in, "out_grad": out_grad, "routes": routes, "block_order": block_order, "norm_attn": norm_attn, "w_query": w_query, "w_kv_down": w_kv_down, "norm_latent": norm_latent, "w_key_up": w_key_up, "w_value_up": w_value_up, "w_out": w_out, "norm_ffn": norm_ffn, "w_router": w_router, "shared_gate": shared_gate, "shared_up": shared_up, "shared_down": shared_down, "expert_gate": expert_gate, "expert_up": expert_up, "expert_down": expert_down}


EPSILON = 1e-06
HIGHEST = lax.Precision.HIGHEST

@jax.custom_vjp
def low(v):
    return lax.optimization_barrier(v.astype(jnp.bfloat16)).astype(jnp.float32)

@jax.custom_vjp
def low_back(v):
    return v

def low_keep(v):
    return (low(v), None)

def low_pass(kept, grad):
    return (grad,)

def back_keep(v):
    return (v, None)

def back_low(kept, grad):
    return (low(grad),)
low.defvjp(low_keep, low_pass)
low_back.defvjp(back_keep, back_low)

def matmul(inputs, matrix):
    return jnp.dot(inputs, matrix, precision=HIGHEST)

def rms_norm(inputs, gain_vec):
    return inputs * lax.rsqrt(lax.optimization_barrier(jnp.mean(inputs * inputs, axis=-1, keepdims=True)) + EPSILON) * gain_vec

def rotate(vectors, angles):
    half_width = vectors.shape[-1] // 2
    first_half = vectors[..., :half_width]
    second_half = vectors[..., half_width:]
    cosine = jnp.cos(angles)
    sine_value = jnp.sin(angles)
    return jnp.concatenate([first_half * cosine - second_half * sine_value, second_half * cosine + first_half * sine_value], axis=-1)

def row_positions(block_order):
    half_rows = LENGTH // HALVES
    row_ids = jnp.arange(LENGTH, dtype=jnp.int32)
    matches = (row_ids // half_rows)[:, None] == jnp.arange(HALVES, dtype=jnp.int32)[None, :]
    starts = lax.optimization_barrier(jnp.sum(jnp.where(matches[None, :, :], block_order[:, None, :], 0), axis=2))
    return (starts * half_rows + row_ids % half_rows).astype(jnp.int32)

def rope_angles(positions):
    inverse = 10000.0 ** (-2.0 * jnp.arange(ROPE // 2, dtype=jnp.float32) / ROPE)
    return positions.astype(jnp.float32)[..., None] * inverse

def reference(hidden_in, out_grad, routes, block_order, norm_attn, w_query, w_kv_down, norm_latent, w_key_up, w_value_up, w_out, norm_ffn, w_router, shared_gate, shared_up, shared_down, expert_gate, expert_up, expert_down):
    positions = row_positions(block_order)
    angles = rope_angles(positions)
    span_rows = LENGTH // N_CTX
    score_scale = (NOPE + ROPE) ** (-0.5)
    route_hot = routes[..., None] == jnp.arange(EXPERTS, dtype=jnp.int32)

    def forward(inputs, gain_attn, query_w, kv_down_w, gain_latent, key_up_w, value_up_w, out_w, gain_ffn, router_w, sh_gate_w, sh_up_w, sh_down_w, ex_gate_w, ex_up_w, ex_down_w):
        normed_attn = low(rms_norm(inputs, gain_attn))
        query_raw = low_back(matmul(normed_attn, query_w)).reshape(SEQS, LENGTH, HEADS, NOPE + ROPE)
        query_rot = rotate(query_raw[..., NOPE:], angles[:, :, None, :])
        queries = low(jnp.concatenate([query_raw[..., :NOPE], query_rot], axis=-1))
        kv_joint = low_back(matmul(normed_attn, kv_down_w))
        latent = low(rms_norm(kv_joint[..., :LATENT], gain_latent))
        key_rope = low(rotate(kv_joint[..., LATENT:], angles))
        key_nope = low(matmul(latent, key_up_w)).reshape(SEQS, LENGTH, HEADS, NOPE)
        values = low(matmul(latent, value_up_w)).reshape(SEQS, LENGTH, HEADS, VDIM)

        def attend(block_id):
            seq_id = block_id // N_CTX
            row_start = block_id % N_CTX * span_rows
            query_block = lax.dynamic_slice_in_dim(queries[seq_id], row_start, span_rows, 0)
            query_pos = lax.dynamic_slice_in_dim(positions[seq_id], row_start, span_rows, 0)
            key_block = low_back(key_nope[seq_id])
            value_block = low_back(values[seq_id])
            raw_scores = jnp.einsum('qhd,khd->hqk', query_block[..., :NOPE], key_block, precision=HIGHEST) + jnp.einsum('qhd,kd->hqk', query_block[..., NOPE:], key_rope[seq_id], precision=HIGHEST)
            scores = low_back(raw_scores) * score_scale
            allowed = positions[seq_id][None, None, :] <= query_pos[None, :, None]
            weights_attn = low(jax.nn.softmax(jnp.where(allowed, scores, -jnp.inf), axis=-1))
            return jnp.einsum('hqk,khd->qhd', weights_attn, value_block, precision=HIGHEST)
        attended = lax.map(jax.checkpoint(attend), jnp.arange(SEQS * N_CTX, dtype=jnp.int32))
        heads_out = low(low_back(attended.reshape(SEQS, LENGTH, HEADS * VDIM)))
        residual = inputs + low_back(matmul(heads_out, out_w))
        normed_ffn = low(rms_norm(residual, gain_ffn))
        logits = low_back(matmul(normed_ffn, router_w))
        chosen = lax.optimization_barrier(jnp.sum(jnp.where(route_hot, logits[:, :, None, :], 0.0), axis=-1))
        gate_weights = jax.nn.softmax(chosen, axis=-1)
        combine = lax.optimization_barrier(jnp.sum(jnp.where(route_hot, gate_weights[..., None], 0.0), axis=2))
        shared_gate_v = low_back(matmul(normed_ffn, sh_gate_w))
        shared_up_v = low_back(matmul(normed_ffn, sh_up_w))
        shared_out = matmul(low(jax.nn.silu(shared_gate_v) * shared_up_v), sh_down_w)
        flat_tokens = normed_ffn.reshape(SEQS * LENGTH, D)

        def expert(running, expert_item):
            gate_w, up_w, down_w, weight = expert_item
            token_rows = low_back(flat_tokens)
            gate_v = low_back(matmul(token_rows, gate_w))
            up_v = low_back(matmul(token_rows, up_w))
            result = low(low_back(matmul(low(jax.nn.silu(gate_v) * up_v), down_w)))
            return (running + weight[:, None] * result, None)
        routed, unused = lax.scan(jax.checkpoint(expert), jnp.zeros_like(flat_tokens), (ex_gate_w, ex_up_w, ex_down_w, combine.reshape(SEQS * LENGTH, EXPERTS).T))
        moe_out = low_back(shared_out + routed.reshape(SEQS, LENGTH, D))
        return residual + moe_out
    float_args = (hidden_in.astype(jnp.float32), norm_attn.astype(jnp.float32), w_query.astype(jnp.float32), w_kv_down.astype(jnp.float32), norm_latent.astype(jnp.float32), w_key_up.astype(jnp.float32), w_value_up.astype(jnp.float32), w_out.astype(jnp.float32), norm_ffn.astype(jnp.float32), w_router.astype(jnp.float32), shared_gate.astype(jnp.float32), shared_up.astype(jnp.float32), shared_down.astype(jnp.float32), expert_gate.astype(jnp.float32), expert_up.astype(jnp.float32), expert_down.astype(jnp.float32))
    output, pullback = jax.vjp(forward, *float_args)
    gradients = pullback(out_grad.astype(jnp.float32))
    return (output.astype(jnp.bfloat16), gradients[0].astype(jnp.bfloat16), gradients[1], gradients[2], gradients[3], gradients[4], gradients[5], gradients[6], gradients[7], gradients[8], gradients[9], gradients[10], gradients[11], gradients[12], gradients[13], gradients[14], gradients[15])
```

```python
import functools

import jax
import jax.numpy as jnp
from jax import lax
from jax.experimental import pallas as pl
from jax.experimental.pallas import tpu as pltpu
from jax.sharding import PartitionSpec as P

NOPE = 128
ROPE = 64
VDIM = 128
LATENT = 512
TOP = 6
EPSILON = 1e-06
MASKED = -1e30
BF16 = jnp.bfloat16
F32 = jnp.float32


def product(inputs, matrix):
    return jnp.dot(inputs, matrix, preferred_element_type=F32)


def back_product(gradient, matrix):
    return lax.dot_general(
        gradient,
        matrix,
        (((gradient.ndim - 1,), (1,)), ((), ())),
        preferred_element_type=F32,
    )


def weight_grad(inputs, gradient):
    flat_in = inputs.reshape(-1, inputs.shape[-1])
    flat_grad = gradient.reshape(-1, gradient.shape[-1])
    return lax.dot_general(
        flat_in, flat_grad, (((0,), (0,)), ((), ())), preferred_element_type=F32
    )


def rope_tables(positions):
    inverse = 10000.0 ** (-2.0 * jnp.arange(ROPE // 2, dtype=F32) / ROPE)
    angles = positions.astype(F32)[..., None] * inverse
    return jnp.cos(angles), jnp.sin(angles)


def halves(vectors):
    return vectors[..., : ROPE // 2], vectors[..., ROPE // 2 :]


def rotate(vectors, tables):
    first, second = halves(vectors)
    cosine, sine = tables
    return jnp.concatenate(
        [first * cosine - second * sine, second * cosine + first * sine], axis=-1
    )


def unrotate(gradient, tables):
    first, second = halves(gradient)
    cosine, sine = tables
    return jnp.concatenate(
        [first * cosine + second * sine, second * cosine - first * sine], axis=-1
    )


def norm_back(gradient, inputs, inverse_rms, gain_vec):
    scaled = gradient * gain_vec
    return inverse_rms * scaled - inputs * inverse_rms**3 * jnp.mean(
        inputs * scaled, axis=-1, keepdims=True
    )


def silu_grads(grad_hidden, gate, upward):
    sigmoid_gate = jax.nn.sigmoid(gate)
    grad_gate = grad_hidden * upward * sigmoid_gate * (1.0 + gate * (1.0 - sigmoid_gate))
    grad_upward = grad_hidden * gate * sigmoid_gate
    return (grad_gate.astype(BF16), grad_upward.astype(BF16))


def dot_nt(left, right):
    return lax.dot_general(left, right, (((1,), (1,)), ((), ())), preferred_element_type=F32)


def dot_tn(left, right):
    return lax.dot_general(left, right, (((0,), (0,)), ((), ())), preferred_element_type=F32)


def dot_nn(left, right):
    return lax.dot_general(left, right, (((1,), (0,)), ((), ())), preferred_element_type=F32)


def head_cols(head):
    return slice(head * NOPE, (head + 1) * NOPE)


def rope_cols(heads, head):
    start = heads * NOPE + head * ROPE
    return slice(start, start + ROPE)


def forward_kernel(heads, scale, q_ref, k_ref, v_ref, kr_ref, pq_ref, pk_ref, o_ref, lse_ref):
    allowed = pk_ref[0] <= pq_ref[0]
    for head in range(heads):
        cols = head_cols(head)
        scores = dot_nt(k_ref[0, :, cols], q_ref[0, :, cols])
        scores = scores + dot_nt(kr_ref[0, :, :ROPE], q_ref[0, :, rope_cols(heads, head)])
        scores = jnp.where(allowed, scores * scale, MASKED)
        top = jnp.max(scores, axis=0, keepdims=True)
        weights = jnp.exp(scores - top)
        total = jnp.sum(weights, axis=0, keepdims=True)
        lse_ref[0, head : head + 1, :] = top + jnp.log(total)
        probs = (weights * (1.0 / total)).astype(BF16)
        o_ref[0, :, cols] = dot_tn(probs, v_ref[0, :, cols]).astype(BF16)


def backward_kernel(
    heads,
    scale,
    q_ref,
    k_ref,
    v_ref,
    kr_ref,
    do_ref,
    lse_ref,
    pq_ref,
    pk_ref,
    dqn_ref,
    dqr_ref,
    dk_ref,
    dv_ref,
    dkr_ref,
    dk_acc,
    dv_acc,
    dkr_acc,
):
    step = pl.program_id(1)

    @pl.when(step == 0)
    def _():
        dk_acc[...] = jnp.zeros_like(dk_acc)
        dv_acc[...] = jnp.zeros_like(dv_acc)
        dkr_acc[...] = jnp.zeros_like(dkr_acc)

    allowed = pk_ref[0] <= pq_ref[0]
    for head in range(heads):
        cols = head_cols(head)
        keys = k_ref[0, :, cols]
        query = q_ref[0, :, cols]
        query_rope = q_ref[0, :, rope_cols(heads, head)]
        grad = do_ref[0, :, cols]
        scores = dot_nt(keys, query) + dot_nt(kr_ref[0, :, :ROPE], query_rope)
        probs = jnp.where(
            allowed, jnp.exp(scores * scale - lse_ref[0, head : head + 1, :]), 0.0
        )
        grad_probs = dot_nt(v_ref[0, :, cols], grad)
        inner = jnp.sum(probs * grad_probs, axis=0, keepdims=True)
        grad_raw = (probs * (grad_probs - inner) * scale).astype(BF16)
        dv_acc[:, cols] += dot_nn(probs.astype(BF16), grad)
        dk_acc[:, cols] += dot_nn(grad_raw, query)
        dkr_acc[...] += dot_nn(grad_raw, query_rope)
        dqn_ref[0, :, cols] = dot_tn(grad_raw, keys).astype(BF16)
        dqr_ref[0, :, cols] = dot_tn(grad_raw, kr_ref[0])

    @pl.when(step == pl.num_programs(1) - 1)
    def _():
        dk_ref[0] = dk_acc[...].astype(BF16)
        dv_ref[0] = dv_acc[...].astype(BF16)
        dkr_ref[0] = dkr_acc[...]


def query_tile(rows, total_rows):
    return min(rows, max(128, 256 * 1024 // total_rows))


def attend(queries, keys, values, key_rope, pos_q, pos_k, heads, scale):
    seqs, rows, width = queries.shape
    total_rows = keys.shape[1]
    tile = query_tile(rows, total_rows)
    flat = heads * NOPE
    return pl.pallas_call(
        functools.partial(forward_kernel, heads, scale),
        grid=(seqs, rows // tile),
        in_specs=[
            pl.BlockSpec((1, tile, width), lambda s, i: (s, i, 0)),
            pl.BlockSpec((1, total_rows, flat), lambda s, i: (s, 0, 0)),
            pl.BlockSpec((1, total_rows, flat), lambda s, i: (s, 0, 0)),
            pl.BlockSpec((1, total_rows, 2 * ROPE), lambda s, i: (s, 0, 0)),
            pl.BlockSpec((1, 1, tile), lambda s, i: (s, 0, i)),
            pl.BlockSpec((1, total_rows, 1), lambda s, i: (s, 0, 0)),
        ],
        out_specs=[
            pl.BlockSpec((1, tile, flat), lambda s, i: (s, i, 0)),
            pl.BlockSpec((1, heads, tile), lambda s, i: (s, 0, i)),
        ],
        out_shape=[
            jax.ShapeDtypeStruct((seqs, rows, flat), BF16),
            jax.ShapeDtypeStruct((seqs, heads, rows), F32),
        ],
        cost_estimate=pl.CostEstimate(
            flops=2 * seqs * heads * rows * total_rows * (NOPE + ROPE + VDIM),
            transcendentals=seqs * heads * rows * total_rows,
            bytes_accessed=2 * seqs * (rows * width + 2 * total_rows * flat),
        ),
        name="attend",
    )(queries, keys, values, key_rope, pos_q[:, None, :], pos_k[:, :, None])


def attend_back(queries, keys, values, key_rope, grads, lse, pos_q, pos_k, heads, scale):
    seqs, rows, width = queries.shape
    total_rows = keys.shape[1]
    tile = query_tile(rows, total_rows)
    flat = heads * NOPE
    whole = lambda s, i: (s, 0, 0)
    piece = lambda s, i: (s, i, 0)
    return pl.pallas_call(
        functools.partial(backward_kernel, heads, scale),
        grid=(seqs, rows // tile),
        in_specs=[
            pl.BlockSpec((1, tile, width), piece),
            pl.BlockSpec((1, total_rows, flat), whole),
            pl.BlockSpec((1, total_rows, flat), whole),
            pl.BlockSpec((1, total_rows, 2 * ROPE), whole),
            pl.BlockSpec((1, tile, flat), piece),
            pl.BlockSpec((1, heads, tile), lambda s, i: (s, 0, i)),
            pl.BlockSpec((1, 1, tile), lambda s, i: (s, 0, i)),
            pl.BlockSpec((1, total_rows, 1), whole),
        ],
        out_specs=[
            pl.BlockSpec((1, tile, flat), piece),
            pl.BlockSpec((1, tile, flat), piece),
            pl.BlockSpec((1, total_rows, flat), whole),
            pl.BlockSpec((1, total_rows, flat), whole),
            pl.BlockSpec((1, total_rows, ROPE), whole),
        ],
        out_shape=[
            jax.ShapeDtypeStruct((seqs, rows, flat), BF16),
            jax.ShapeDtypeStruct((seqs, rows, flat), F32),
            jax.ShapeDtypeStruct((seqs, total_rows, flat), BF16),
            jax.ShapeDtypeStruct((seqs, total_rows, flat), BF16),
            jax.ShapeDtypeStruct((seqs, total_rows, ROPE), F32),
        ],
        scratch_shapes=[
            pltpu.VMEM((total_rows, flat), F32),
            pltpu.VMEM((total_rows, flat), F32),
            pltpu.VMEM((total_rows, ROPE), F32),
        ],
        cost_estimate=pl.CostEstimate(
            flops=4 * seqs * heads * rows * total_rows * (NOPE + ROPE + VDIM),
            transcendentals=seqs * heads * rows * total_rows,
            bytes_accessed=2 * seqs * (rows * width + 4 * total_rows * flat),
        ),
        name="attend_back",
    )(queries, keys, values, key_rope, grads, lse, pos_q[:, None, :], pos_k[:, :, None])


def shards(
    hidden_in,
    out_grad,
    routes,
    block_order,
    norm_attn,
    w_query,
    w_kv_down,
    norm_latent,
    w_key_up,
    w_value_up,
    w_out,
    norm_ffn,
    w_router,
    shared_gate,
    shared_up,
    shared_down,
    expert_gate,
    expert_up,
    expert_down,
):
    seqs, piece, width = hidden_in.shape
    n_expert = lax.axis_size("expert")
    n_ctx = lax.axis_size("ctx")
    n_dp = lax.axis_size("dp")
    lanes = n_expert // 2
    heads = w_query.shape[1] // (NOPE + ROPE)
    expert_count = w_router.shape[1]
    slots = 8 * ((piece * TOP + 6 * expert_count - 1) // (6 * expert_count))
    expert_rank = lax.axis_index("expert")
    ctx_rank = lax.axis_index("ctx")
    dp_rank = lax.axis_index("dp")
    span = piece * n_expert
    total_rows = span * n_ctx
    scale = (NOPE + ROPE) ** (-0.5)
    group = lanes * piece
    group_slots = lanes * slots

    def shift(value, steps):
        pairs = [(e, (e + 2 * steps) % n_expert) for e in range(n_expert)]
        return lax.ppermute(value, "expert", pairs)

    def across(value):
        return lax.ppermute(value, "expert", [(e, e ^ 1) for e in range(n_expert)])

    def other_dp(value):
        return lax.ppermute(value, "dp", [(d, n_dp - 1 - d) for d in range(n_dp)])

    def other_ctx(value):
        return lax.ppermute(value, "ctx", [(c, n_ctx - 1 - c) for c in range(n_ctx)])

    up_count = lanes // 2
    down_count = lanes - 1 - up_count

    def gather_blocks(own):
        other = [across(own)]
        ups, downs = [own], [own]
        for k in range(max(up_count, down_count)):
            if k < up_count:
                ups.append(shift(ups[-1], 1))
            if k < down_count:
                downs.append(shift(downs[-1], -1))
        column = ups + downs[:0:-1]
        return column + other + [across(b) for b in column[1:]]

    def add(*terms):
        total = terms[0].astype(F32)
        for term in terms[1:]:
            total = total + term.astype(F32)
        return total.astype(BF16)

    def scatter_blocks(part):
        order = [up_count] + [k for k in range(lanes - 1, 0, -1) if k != up_count] + [0]
        crossed = {k: across(part(lanes + k)) for k in order}
        sums = {k: (part(k), crossed[k]) for k in order}
        moving = add(*sums[up_count])
        for k in range(up_count, 0, -1):
            moving = shift(moving, -1)
            if k > 1:
                moving = add(*sums[k - 1], moving)
        result = [*sums[0], moving]
        if down_count:
            moving = add(*sums[lanes - down_count])
            for d in range(down_count, 0, -1):
                moving = shift(moving, 1)
                if d > 1:
                    moving = add(*sums[lanes - d + 1], moving)
            result.append(moving)
        return sum(term.astype(F32) for term in result)

    def sum_copies(grad):
        sent = grad.astype(BF16)
        if n_ctx != 2:
            return lax.psum(sent, ("dp", "ctx")).astype(F32)
        half = grad.shape[0] // 2
        mine = lax.dynamic_slice_in_dim(sent, ctx_rank * half, half, 0)
        theirs = lax.dynamic_slice_in_dim(sent, (1 - ctx_rank) * half, half, 0)
        pair = add(mine, other_ctx(theirs))
        full = add(pair, other_dp(pair))
        rest = other_ctx(full)
        first = ctx_rank == 0
        return jnp.concatenate(
            [jnp.where(first, full, rest), jnp.where(first, rest, full)], axis=0
        ).astype(F32)

    def split_copies(grad):
        sent = grad.astype(BF16)
        if n_ctx != 2:
            return lax.psum_scatter(sent, "ctx", scatter_dimension=0, tiled=True).astype(F32)
        half = grad.shape[0] // 2
        theirs = lax.dynamic_slice_in_dim(sent, (1 - ctx_rank) * half, half, 0)
        mine = lax.dynamic_slice_in_dim(sent, ctx_rank * half, half, 0)
        return mine.astype(F32) + other_ctx(theirs).astype(F32)

    rank_z, rank_x = expert_rank // 2, expert_rank % 2
    owners = [
        ((rank_z - j % lanes) % lanes) * 2 + (rank_x + j // lanes) % 2 for j in range(n_expert)
    ]
    owner_ids = jnp.stack(owners)
    ids = jnp.arange(n_expert, dtype=jnp.int32)
    block_of = ((ids % 2 + rank_x) % 2) * lanes + (rank_z - ids // 2) % lanes

    half_rows = total_rows // (2 * n_ctx)

    def positions(row_ids):
        matches = (row_ids // half_rows)[:, None] == jnp.arange(2 * n_ctx, dtype=jnp.int32)
        starts = jnp.sum(jnp.where(matches[None], block_order[:, None, :], 0), axis=2)
        return starts * half_rows + row_ids % half_rows

    row_ids = jnp.arange(total_rows, dtype=jnp.int32)
    all_pos = positions(row_ids)
    piece_ids = jnp.arange(piece, dtype=jnp.int32)
    span_ids = (ctx_rank * span + owner_ids[:, None] * piece + piece_ids[None, :]).reshape(-1)
    span_pos = positions(span_ids)
    own_tables = rope_tables(span_pos[:, :piece])
    span_cos, span_sin = rope_tables(span_pos)
    span_cos = jnp.tile(span_cos, (1, 1, 2 * heads))
    span_sin = jnp.tile(span_sin, (1, 1, 2 * heads))

    blocks = gather_blocks(hidden_in)
    copies = n_dp * n_ctx
    kv_rows = w_kv_down.shape[0]
    kv_piece = kv_rows // copies
    copy_rank = dp_rank * n_ctx + ctx_rank
    kv_all = lax.all_gather(
        lax.dynamic_slice_in_dim(w_kv_down, copy_rank * kv_piece, kv_piece, 0),
        ("dp", "ctx", "expert"),
        axis=0,
        tiled=True,
    )
    kv_full = (
        kv_all.reshape(copies, n_expert, kv_piece, -1).transpose(1, 0, 2, 3).reshape(width, -1)
    )
    routes_all = lax.all_gather(routes.reshape(-1), "expert", axis=0)

    def rms(rows):
        return lax.rsqrt(jnp.mean(rows * rows, axis=-1, keepdims=True) + EPSILON)

    own_rows = hidden_in.astype(F32)
    inv_own = rms(own_rows)
    unit_own = own_rows * inv_own
    normed_own = (unit_own * norm_attn).astype(BF16)
    kv_joint = product(normed_own, kv_full)
    latent_raw = kv_joint[..., :LATENT]
    inv_latent = rms(latent_raw)
    unit_latent = latent_raw * inv_latent
    latent_own = jnp.concatenate(
        [unit_latent * norm_latent, rotate(kv_joint[..., LATENT:], own_tables)], axis=-1
    ).astype(BF16)
    latent_all = lax.all_gather(latent_own, ("ctx", "expert"), axis=1, tiled=True)
    grad_all = lax.all_gather(out_grad, "expert", axis=0)

    per_head = w_query.reshape(width, heads, NOPE + ROPE)
    w_nope = per_head[..., :NOPE].reshape(width, heads * NOPE)
    w_rope = per_head[..., NOPE:]
    first, second = halves(w_rope)
    w_turned = jnp.concatenate([-second, first], axis=-1).reshape(width, heads * ROPE)
    w_inner = jnp.concatenate([w_nope, w_rope.reshape(width, heads * ROPE)], axis=-1)
    input_span = jnp.concatenate(blocks, axis=1).astype(F32)
    inv_span = rms(input_span)
    normed_span = (input_span * inv_span * norm_attn).astype(BF16)
    query_raw = product(normed_span, jnp.concatenate([w_inner, w_turned], axis=-1))
    flat = heads * NOPE
    queries = jnp.concatenate(
        [
            query_raw[..., :flat],
            query_raw[..., flat : flat + heads * ROPE] * span_cos
            + query_raw[..., flat + heads * ROPE :] * span_sin,
        ],
        axis=-1,
    ).astype(BF16)
    latent_part = latent_all[..., :LATENT]
    key_rope = latent_all[..., LATENT:]
    rope_first, rope_second = halves(key_rope)
    key_rope = jnp.concatenate([key_rope, rope_second, -rope_first], axis=-1)
    keys = product(latent_part, w_key_up).astype(BF16)
    values = product(latent_part, w_value_up).astype(BF16)
    heads_out, lse = attend(
        queries, keys, values, key_rope, span_pos, all_pos, heads, scale
    )

    def block_of_span(array, j):
        return array[:, j * piece : (j + 1) * piece]

    attn_own = scatter_blocks(
        lambda j: product(block_of_span(heads_out, j), w_out).astype(BF16)
    )
    residual = own_rows + attn_own
    inv_ffn = rms(residual)
    unit_ffn = residual * inv_ffn
    normed_ffn = (unit_ffn * norm_ffn).astype(BF16)

    grad_span = jnp.concatenate(
        [lax.dynamic_index_in_dim(grad_all, owners[j], 0, False) for j in range(n_expert)], axis=1
    )
    routes_span = jnp.take(
        routes_all.reshape(n_expert, seqs, piece, TOP), owner_ids, axis=0
    ).transpose(1, 0, 2, 3)
    mine = dp_rank * n_expert + expert_rank
    theirs = (n_dp - 1 - dp_rank) * n_expert + expert_rank
    earlier = (piece_ids[:, None] < piece_ids[None, :]).astype(F32)
    lane_ids = jnp.arange(lanes, dtype=jnp.int32)
    hits, picks = [], []
    for target in (mine, theirs):
        hit = routes_span == target
        named = jnp.any(hit, axis=-1)
        rank = jnp.einsum("sjp,pq->sjq", named.astype(F32), earlier).astype(jnp.int32)
        slot = jnp.where(
            named.reshape(seqs, 2, lanes, piece),
            rank.reshape(seqs, 2, lanes, piece) + lane_ids[:, None] * slots,
            -1,
        ).reshape(seqs, 2, 1, group)
        hits.append(hit.reshape(seqs, span, TOP))
        picks.append(slot == jnp.arange(group_slots, dtype=jnp.int32)[:, None])
    picks_bf = [pick.astype(BF16) for pick in picks]

    def pick_rows(pick, rows):
        return jnp.einsum(
            "sgmr,sgrd->sgmd",
            pick,
            rows.reshape(seqs, 2, group, width),
            preferred_element_type=F32,
        ).astype(BF16)

    def place_rows(pick, rows):
        return jnp.einsum("sgmr,sgmd->sgrd", pick, rows, preferred_element_type=F32)

    grad_slots = pick_rows(picks_bf[0], grad_span)
    grad_got = other_dp(pick_rows(picks_bf[1], grad_span))

    ffn_span = jnp.concatenate(gather_blocks(normed_ffn), axis=1)
    token_slots = pick_rows(picks_bf[0], ffn_span)
    token_got = other_dp(pick_rows(picks_bf[1], ffn_span))
    logits_span = product(ffn_span, w_router)
    hot_span = routes_span.reshape(seqs, span, TOP)[..., None] == jnp.arange(
        expert_count, dtype=jnp.int32
    )
    chosen_span = jnp.sum(jnp.where(hot_span, logits_span[:, :, None, :], 0.0), axis=-1)
    gates_span = jax.nn.softmax(chosen_span, axis=-1)
    row_gates = [
        jnp.sum(jnp.where(hit, gates_span, 0.0), axis=-1).reshape(seqs, 2, 1, group)
        for hit in hits
    ]
    gated = [jnp.where(pick, gate, 0.0) for pick, gate in zip(picks, row_gates)]
    slot_gates = [jnp.sum(weights, axis=-1) for weights in gated]
    gates_got = other_dp(slot_gates[1])

    sh_gate = product(ffn_span, shared_gate)
    sh_up = product(ffn_span, shared_up)
    sh_hidden = (jax.nn.silu(sh_gate) * sh_up).astype(BF16)
    sh_dgate, sh_dup = silu_grads(back_product(grad_span, shared_down), sh_gate, sh_up)

    half_slots = seqs * 2 * group_slots
    rows_in = jnp.concatenate([token_slots, token_got], axis=0).reshape(-1, width)
    grads_raw = jnp.concatenate([grad_slots, grad_got], axis=0).reshape(-1, width)
    gates_in = jnp.concatenate([slot_gates[0], gates_got], axis=0).reshape(-1, 1)
    grads_in = (grads_raw.astype(F32) * gates_in).astype(BF16)
    ex_gate = product(rows_in, expert_gate[0])
    ex_up = product(rows_in, expert_up[0])
    ex_hidden = (jax.nn.silu(ex_gate) * ex_up).astype(BF16)
    ex_out = product(ex_hidden, expert_down[0]).astype(BF16)
    grad_gate, grad_upward = silu_grads(back_product(grads_in, expert_down[0]), ex_gate, ex_up)
    ex_dx = (
        back_product(grad_gate, expert_gate[0]) + back_product(grad_upward, expert_up[0])
    ).astype(BF16)
    dg_slots = jnp.sum(grads_raw.astype(F32) * ex_out.astype(F32), axis=-1)

    def sides(array):
        shape = (seqs, 2, group_slots) + array.shape[1:]
        return array[:half_slots].reshape(shape), other_dp(array[half_slots:].reshape(shape))

    dx_sides = sides(ex_dx)
    dg_sides = sides(dg_slots)
    out_sides = sides(ex_out)

    dg_rows = jnp.stack(
        [
            jnp.sum(jnp.where(pick, dg[..., None], 0.0), axis=2).reshape(seqs, n_expert, piece)
            for pick, dg in zip(picks, dg_sides)
        ]
    )
    dg_all = lax.all_gather(jnp.take(dg_rows, block_of, axis=2), "expert", axis=0)
    dg_own = lax.dynamic_index_in_dim(dg_all, expert_rank, 3, False)
    dg_near, dg_far = dg_own[:, 0], dg_own[:, 1]
    first_dp = dp_rank == 0
    dg_own = jnp.concatenate(
        [jnp.where(first_dp, dg_near, dg_far), jnp.where(first_dp, dg_far, dg_near)], axis=0
    ).transpose(1, 2, 0)

    dnorm_part = (
        back_product(sh_dgate, shared_gate)
        + back_product(sh_dup, shared_up)
        + sum(place_rows(p, dx) for p, dx in zip(picks_bf, dx_sides)).reshape(seqs, span, width)
    ).astype(BF16)
    dnorm_sum = scatter_blocks(lambda j: block_of_span(dnorm_part, j))
    route_hot = routes[..., None] == jnp.arange(expert_count, dtype=jnp.int32)
    logits = product(normed_ffn, w_router)
    chosen = jnp.sum(jnp.where(route_hot, logits[:, :, None, :], 0.0), axis=-1)
    gate_weights = jax.nn.softmax(chosen, axis=-1)
    grad_choice = jnp.sum(jnp.where(route_hot, dg_own[:, :, None, :], 0.0), axis=-1)
    grad_chosen = gate_weights * (
        grad_choice - jnp.sum(gate_weights * grad_choice, axis=-1, keepdims=True)
    )
    grad_logits = jnp.sum(jnp.where(route_hot, grad_chosen[..., None], 0.0), axis=2).astype(BF16)
    dnorm_ffn = dnorm_sum + back_product(grad_logits, w_router)
    grad_router = weight_grad(normed_ffn, grad_logits)
    grad_gain_ffn = jnp.sum(dnorm_ffn * unit_ffn, axis=(0, 1))
    grad_resid = out_grad.astype(F32) + norm_back(dnorm_ffn, residual, inv_ffn, norm_ffn)
    grad_attn = jnp.concatenate(gather_blocks(grad_resid.astype(BF16)), axis=1)

    out_part = (
        product(sh_hidden, shared_down)
        + sum(place_rows(p.astype(BF16), o) for p, o in zip(gated, out_sides)).reshape(
            seqs, span, width
        )
    ).astype(BF16)
    out_part = jnp.take(out_part.reshape(seqs, n_expert, piece, width), block_of, axis=1)
    out_own = lax.psum_scatter(out_part, "expert", scatter_dimension=1, tiled=False)
    out_hidden = (residual + out_own.astype(F32)).astype(BF16)

    exp_grads = (
        split_copies(weight_grad(rows_in, grad_gate))[None],
        split_copies(weight_grad(rows_in, grad_upward))[None],
        split_copies(weight_grad(ex_hidden, grads_in))[None],
    )
    grad_sh_in = sum_copies(weight_grad(ffn_span, jnp.concatenate([sh_dgate, sh_dup], axis=-1)))
    grad_sh_down = sum_copies(weight_grad(sh_hidden, grad_span))
    shared_width = shared_gate.shape[1]

    grad_heads = back_product(grad_attn, w_out).astype(BF16)
    grad_out_w = sum_copies(weight_grad(heads_out, grad_attn))
    dq_nope, dq_rope, grad_keys, grad_values, grad_key_rope = attend_back(
        queries, keys, values, key_rope, grad_heads, lse, span_pos, all_pos, heads, scale
    )
    dq_rope = dq_rope.reshape(seqs, span, heads, 2, ROPE)
    turned = (
        dq_rope[..., 0, :] * span_cos[..., None, :ROPE]
        + dq_rope[..., 1, :] * span_sin[..., None, :ROPE]
    )
    grad_queries = jnp.concatenate(
        [dq_nope, turned.reshape(seqs, span, heads * ROPE).astype(BF16)], axis=-1
    )
    grad_latent = jnp.concatenate(
        [
            back_product(grad_keys, w_key_up) + back_product(grad_values, w_value_up),
            grad_key_rope,
        ],
        axis=-1,
    ).astype(BF16)
    grad_latent_own = lax.psum_scatter(
        grad_latent, ("ctx", "expert"), scatter_dimension=1, tiled=True
    ).astype(F32)
    dnorm_query = back_product(grad_queries, w_inner)
    dnorm_parts = dnorm_query.astype(BF16)
    dnorm_own = scatter_blocks(lambda j: block_of_span(dnorm_parts, j))
    gain_part = jnp.sum(dnorm_query * (input_span * inv_span), axis=(0, 1))
    grad_query_in = sum_copies(weight_grad(normed_span, grad_queries))
    grad_up = weight_grad(latent_part, jnp.concatenate([grad_keys, grad_values], axis=-1))
    grad_up = sum_copies(grad_up)

    grad_unit = grad_latent_own[..., :LATENT]
    grad_gain_latent = jnp.sum(grad_unit * unit_latent, axis=(0, 1))
    grad_kv = jnp.concatenate(
        [
            norm_back(grad_unit, latent_raw, inv_latent, norm_latent),
            unrotate(grad_latent_own[..., LATENT:], own_tables),
        ],
        axis=-1,
    ).astype(BF16)
    grad_kv_all = jnp.take(lax.all_gather(grad_kv, "expert", axis=0), owner_ids, axis=0)
    normed_cols = lax.dynamic_slice_in_dim(normed_span, expert_rank * kv_rows, kv_rows, 2)
    grad_kv_w = sum_copies(
        weight_grad(
            normed_cols, grad_kv_all.transpose(1, 0, 2, 3).reshape(seqs, span, -1)
        )
    )
    dnorm_kv = back_product(grad_kv, kv_full)
    gain_part = gain_part + jnp.sum(dnorm_kv * unit_own, axis=(0, 1))
    in_grad = (
        grad_resid + norm_back(dnorm_own + dnorm_kv, own_rows, inv_own, norm_attn)
    ).astype(BF16)

    def by_rank(array):
        return array.reshape(n_expert, -1)

    small = jnp.concatenate(
        [by_rank(gain_part), by_rank(grad_gain_latent), by_rank(grad_gain_ffn), by_rank(grad_router)],
        axis=1,
    )
    small = lax.psum(small, ("dp", "ctx", "expert"))
    small = lax.dynamic_index_in_dim(small, expert_rank, 0, False)
    rows = width // n_expert
    latent_rows = LATENT // n_expert
    gain_attn = small[:rows]
    gain_latent = small[rows : rows + latent_rows]
    gain_ffn = small[rows + latent_rows : 2 * rows + latent_rows]
    router = small[2 * rows + latent_rows :].reshape(rows, expert_count)

    grad_query_w = jnp.concatenate(
        [
            grad_query_in[:, :flat].reshape(width, heads, NOPE),
            grad_query_in[:, flat:].reshape(width, heads, ROPE),
        ],
        axis=-1,
    ).reshape(width, heads * (NOPE + ROPE))
    return (
        out_hidden,
        in_grad,
        gain_attn,
        grad_query_w,
        grad_kv_w,
        gain_latent,
        grad_up[:, :flat],
        grad_up[:, flat:],
        grad_out_w,
        gain_ffn,
        router,
        grad_sh_in[:, :shared_width],
        grad_sh_in[:, shared_width:],
        grad_sh_down,
        exp_grads[0],
        exp_grads[1],
        exp_grads[2],
    )


def solution(mesh):
    return jax.shard_map(
        shards,
        mesh=mesh,
        in_specs=(
            P("dp", ("ctx", "expert"), None),
            P("dp", ("ctx", "expert"), None),
            P("dp", ("ctx", "expert"), None),
            P("dp", None),
            P(),
            P(None, "expert"),
            P("expert", None),
            P(),
            P(None, "expert"),
            P(None, "expert"),
            P("expert", None),
            P(),
            P(),
            P(None, "expert"),
            P(None, "expert"),
            P("expert", None),
            P(("dp", "expert"), None, None),
            P(("dp", "expert"), None, None),
            P(("dp", "expert"), None, None),
        ),
        out_specs=(
            P("dp", ("ctx", "expert"), None),
            P("dp", ("ctx", "expert"), None),
            P("expert"),
            P(None, "expert"),
            P("expert", None),
            P("expert"),
            P(None, "expert"),
            P(None, "expert"),
            P("expert", None),
            P("expert"),
            P("expert", None),
            P(None, "expert"),
            P(None, "expert"),
            P("expert", None),
            P(("dp", "expert"), "ctx", None),
            P(("dp", "expert"), "ctx", None),
            P(("dp", "expert"), "ctx", None),
        ),
        check_vma=False,
    )
```

```python
import functools

import jax
import jax.numpy as jnp
from jax import lax
from jax.experimental import pallas as pl
from jax.experimental.pallas import tpu as pltpu
from jax.sharding import PartitionSpec as P

NOPE = 128
ROPE = 64
VDIM = 128
LATENT = 512
TOP = 6
EPSILON = 1e-06
MASKED = -1e30
BF16 = jnp.bfloat16
F32 = jnp.float32


def product(inputs, matrix):
    return jnp.dot(inputs, matrix, preferred_element_type=F32)


def back_product(gradient, matrix):
    return lax.dot_general(
        gradient,
        matrix,
        (((gradient.ndim - 1,), (1,)), ((), ())),
        preferred_element_type=F32,
    )


def weight_grad(inputs, gradient):
    flat_in = inputs.reshape(-1, inputs.shape[-1])
    flat_grad = gradient.reshape(-1, gradient.shape[-1])
    return lax.dot_general(
        flat_in, flat_grad, (((0,), (0,)), ((), ())), preferred_element_type=F32
    )


def rope_tables(positions):
    inverse = 10000.0 ** (-2.0 * jnp.arange(ROPE // 2, dtype=F32) / ROPE)
    angles = positions.astype(F32)[..., None] * inverse
    return jnp.cos(angles), jnp.sin(angles)


def halves(vectors):
    return vectors[..., : ROPE // 2], vectors[..., ROPE // 2 :]


def rotate(vectors, tables):
    first, second = halves(vectors)
    cosine, sine = tables
    return jnp.concatenate(
        [first * cosine - second * sine, second * cosine + first * sine], axis=-1
    )


def unrotate(gradient, tables):
    first, second = halves(gradient)
    cosine, sine = tables
    return jnp.concatenate(
        [first * cosine + second * sine, second * cosine - first * sine], axis=-1
    )


def norm_back(gradient, inputs, inverse_rms, gain_vec):
    scaled = gradient * gain_vec
    return inverse_rms * scaled - inputs * inverse_rms**3 * jnp.mean(
        inputs * scaled, axis=-1, keepdims=True
    )


def silu_grads(grad_hidden, gate, upward):
    sigmoid_gate = jax.nn.sigmoid(gate)
    grad_gate = grad_hidden * upward * sigmoid_gate * (1.0 + gate * (1.0 - sigmoid_gate))
    grad_upward = grad_hidden * gate * sigmoid_gate
    return (grad_gate.astype(BF16), grad_upward.astype(BF16))


def dot_nt(left, right):
    return lax.dot_general(left, right, (((1,), (1,)), ((), ())), preferred_element_type=F32)


def dot_tn(left, right):
    return lax.dot_general(left, right, (((0,), (0,)), ((), ())), preferred_element_type=F32)


def dot_nn(left, right):
    return lax.dot_general(left, right, (((1,), (0,)), ((), ())), preferred_element_type=F32)


def head_cols(head):
    return slice(head * NOPE, (head + 1) * NOPE)


def rope_cols(heads, head):
    start = heads * NOPE + head * ROPE
    return slice(start, start + ROPE)


def forward_kernel(heads, scale, q_ref, k_ref, v_ref, kr_ref, pq_ref, pk_ref, o_ref, lse_ref):
    allowed = pk_ref[0] <= pq_ref[0]
    for head in range(heads):
        cols = head_cols(head)
        scores = dot_nt(k_ref[0, :, cols], q_ref[0, :, cols])
        scores = scores + dot_nt(kr_ref[0, :, :ROPE], q_ref[0, :, rope_cols(heads, head)])
        scores = jnp.where(allowed, scores * scale, MASKED)
        top = jnp.max(scores, axis=0, keepdims=True)
        weights = jnp.exp(scores - top)
        total = jnp.sum(weights, axis=0, keepdims=True)
        lse_ref[0, head : head + 1, :] = top + jnp.log(total)
        probs = (weights * (1.0 / total)).astype(BF16)
        o_ref[0, :, cols] = dot_tn(probs, v_ref[0, :, cols]).astype(BF16)


def backward_kernel(
    heads,
    scale,
    q_ref,
    k_ref,
    v_ref,
    kr_ref,
    do_ref,
    lse_ref,
    pq_ref,
    pk_ref,
    turn_ref,
    dq_ref,
    dkv_ref,
    dkr_ref,
    dkv_acc,
    dkr_acc,
):
    step = pl.program_id(1)

    @pl.when(step == 0)
    def _():
        dkv_acc[...] = jnp.zeros_like(dkv_acc)
        dkr_acc[...] = jnp.zeros_like(dkr_acc)

    allowed = pk_ref[0] <= pq_ref[0]
    pieces = []
    for head in range(heads):
        cols = head_cols(head)
        value_cols = head_cols(heads + head)
        keys = k_ref[0, :, cols]
        query = q_ref[0, :, cols]
        query_rope = q_ref[0, :, rope_cols(heads, head)]
        grad = do_ref[0, :, cols]
        scores = dot_nt(keys, query) + dot_nt(kr_ref[0, :, :ROPE], query_rope)
        probs = jnp.where(
            allowed, jnp.exp(scores * scale - lse_ref[0, head : head + 1, :]), 0.0
        )
        grad_probs = dot_nt(v_ref[0, :, cols], grad)
        inner = jnp.sum(probs * grad_probs, axis=0, keepdims=True)
        grad_raw = (probs * (grad_probs - inner) * scale).astype(BF16)
        dkv_acc[:, value_cols] += dot_nn(probs.astype(BF16), grad)
        dkv_acc[:, cols] += dot_nn(grad_raw, query)
        dkr_acc[...] += dot_nn(grad_raw, query_rope)
        turned = dot_tn(grad_raw, kr_ref[0]) * turn_ref[0]
        pieces.append(dot_tn(grad_raw, keys))
        pieces.append(turned[:, :ROPE] + turned[:, ROPE:])
    dq_ref[0] = jnp.concatenate(pieces, axis=1).astype(BF16)

    @pl.when(step == pl.num_programs(1) - 1)
    def _():
        dkv_ref[0] = dkv_acc[...].astype(BF16)
        dkr_ref[0] = dkr_acc[...].astype(BF16)


def query_tile(rows, total_rows):
    return min(rows, max(128, 256 * 1024 // total_rows))


def attend(queries, pairs, key_rope, pos_q, pos_k, heads, scale):
    seqs, rows, width = queries.shape
    total_rows = pairs.shape[1]
    tile = query_tile(rows, total_rows)
    flat = heads * NOPE
    return pl.pallas_call(
        functools.partial(forward_kernel, heads, scale),
        grid=(seqs, rows // tile),
        in_specs=[
            pl.BlockSpec((1, tile, width), lambda s, i: (s, i, 0)),
            pl.BlockSpec((1, total_rows, flat), lambda s, i: (s, 0, 0)),
            pl.BlockSpec((1, total_rows, flat), lambda s, i: (s, 0, 1)),
            pl.BlockSpec((1, total_rows, 2 * ROPE), lambda s, i: (s, 0, 0)),
            pl.BlockSpec((1, 1, tile), lambda s, i: (s, 0, i)),
            pl.BlockSpec((1, total_rows, 1), lambda s, i: (s, 0, 0)),
        ],
        out_specs=[
            pl.BlockSpec((1, tile, flat), lambda s, i: (s, i, 0)),
            pl.BlockSpec((1, heads, tile), lambda s, i: (s, 0, i)),
        ],
        out_shape=[
            jax.ShapeDtypeStruct((seqs, rows, flat), BF16),
            jax.ShapeDtypeStruct((seqs, heads, rows), F32),
        ],
        cost_estimate=pl.CostEstimate(
            flops=2 * seqs * heads * rows * total_rows * (NOPE + ROPE + VDIM),
            transcendentals=seqs * heads * rows * total_rows,
            bytes_accessed=2 * seqs * (rows * width + 2 * total_rows * flat),
        ),
        name="attend",
    )(queries, pairs, pairs, key_rope, pos_q[:, None, :], pos_k[:, :, None])


def attend_back(queries, pairs, key_rope, grads, lse, pos_q, pos_k, turns, heads, scale):
    seqs, rows, width = queries.shape
    total_rows = pairs.shape[1]
    tile = query_tile(rows, total_rows)
    flat = heads * NOPE
    whole = lambda s, i: (s, 0, 0)
    piece = lambda s, i: (s, i, 0)
    return pl.pallas_call(
        functools.partial(backward_kernel, heads, scale),
        grid=(seqs, rows // tile),
        in_specs=[
            pl.BlockSpec((1, tile, width), piece),
            pl.BlockSpec((1, total_rows, flat), whole),
            pl.BlockSpec((1, total_rows, flat), lambda s, i: (s, 0, 1)),
            pl.BlockSpec((1, total_rows, 2 * ROPE), whole),
            pl.BlockSpec((1, tile, flat), piece),
            pl.BlockSpec((1, heads, tile), lambda s, i: (s, 0, i)),
            pl.BlockSpec((1, 1, tile), lambda s, i: (s, 0, i)),
            pl.BlockSpec((1, total_rows, 1), whole),
            pl.BlockSpec((1, tile, 2 * ROPE), piece),
        ],
        out_specs=[
            pl.BlockSpec((1, tile, width), piece),
            pl.BlockSpec((1, total_rows, 2 * flat), whole),
            pl.BlockSpec((1, total_rows, ROPE), whole),
        ],
        out_shape=[
            jax.ShapeDtypeStruct((seqs, rows, width), BF16),
            jax.ShapeDtypeStruct((seqs, total_rows, 2 * flat), BF16),
            jax.ShapeDtypeStruct((seqs, total_rows, ROPE), BF16),
        ],
        scratch_shapes=[
            pltpu.VMEM((total_rows, 2 * flat), F32),
            pltpu.VMEM((total_rows, ROPE), F32),
        ],
        cost_estimate=pl.CostEstimate(
            flops=4 * seqs * heads * rows * total_rows * (NOPE + ROPE + VDIM),
            transcendentals=seqs * heads * rows * total_rows,
            bytes_accessed=2 * seqs * (rows * width + 4 * total_rows * flat),
        ),
        name="attend_back",
    )(
        queries, pairs, pairs, key_rope, grads, lse, pos_q[:, None, :], pos_k[:, :, None], turns
    )


def join_kernel(count, *refs):
    rows = refs[0].shape[1]
    for j in range(count):
        refs[count][0, j * rows : (j + 1) * rows, :] = refs[j][0]


def join_norm_kernel(count, *refs):
    gain, out = refs[count][...], refs[count + 1]
    rows = refs[0].shape[1]
    for j in range(count):
        values = refs[j][0].astype(F32)
        inverse = lax.rsqrt(jnp.mean(values * values, axis=-1, keepdims=True) + EPSILON)
        out[0, j * rows : (j + 1) * rows, :] = (values * inverse * gain).astype(BF16)


def join(blocks, gain=None):
    seqs, rows, width = blocks[0].shape
    count = len(blocks)
    specs = [pl.BlockSpec((1, rows, width), lambda s: (s, 0, 0))] * count
    operands = list(blocks)
    if gain is not None:
        specs.append(pl.BlockSpec((1, width), lambda s: (0, 0)))
        operands.append(gain[None])
    return pl.pallas_call(
        functools.partial(join_kernel if gain is None else join_norm_kernel, count),
        grid=(seqs,),
        in_specs=specs,
        out_specs=pl.BlockSpec((1, count * rows, width), lambda s: (s, 0, 0)),
        out_shape=jax.ShapeDtypeStruct((seqs, count * rows, width), BF16),
        cost_estimate=pl.CostEstimate(
            flops=0, transcendentals=0, bytes_accessed=4 * seqs * count * rows * width
        ),
        name="join",
    )(*operands)


def pick_kernel(count, slots, *refs):
    near, far = refs[count + 2], refs[count + 3]
    for j in range(count):
        rows = refs[j][0]
        part = slice(j * slots, (j + 1) * slots)
        near[0, part, :] = dot_nn(refs[count][0, part, :], rows).astype(BF16)
        far[0, part, :] = dot_nn(refs[count + 1][0, part, :], rows).astype(BF16)


def pick_blocks(blocks, near, far):
    seqs, rows, width = blocks[0].shape
    count = len(blocks)
    total = near.shape[1]
    block = pl.BlockSpec((1, rows, width), lambda s: (s, 0, 0))
    table = pl.BlockSpec((1, total, rows), lambda s: (s, 0, 0))
    out = pl.BlockSpec((1, total, width), lambda s: (s, 0, 0))
    return pl.pallas_call(
        functools.partial(pick_kernel, count, total // count),
        grid=(seqs,),
        in_specs=[block] * count + [table] * 2,
        out_specs=[out] * 2,
        out_shape=[jax.ShapeDtypeStruct((seqs, total, width), BF16)] * 2,
        cost_estimate=pl.CostEstimate(
            flops=4 * seqs * total * rows * width,
            transcendentals=0,
            bytes_accessed=2 * seqs * (count * rows + 2 * total) * width,
        ),
        name="pick",
    )(*blocks, near, far)


def copy_kernel(index_ref, in_ref, out_ref):
    out_ref[...] = in_ref[...]


def reorder(array, index):
    seqs, total, width = array.shape
    count = index.shape[0]
    rows = total // count
    return pl.pallas_call(
        copy_kernel,
        grid_spec=pltpu.PrefetchScalarGridSpec(
            num_scalar_prefetch=1,
            grid=(seqs, count),
            in_specs=[pl.BlockSpec((1, rows, width), lambda s, j, index: (s, index[j], 0))],
            out_specs=pl.BlockSpec((1, rows, width), lambda s, j, index: (s, j, 0)),
        ),
        out_shape=jax.ShapeDtypeStruct(array.shape, array.dtype),
        cost_estimate=pl.CostEstimate(
            flops=0, transcendentals=0, bytes_accessed=4 * seqs * total * width
        ),
        name="reorder",
    )(index, array)


def spread_kernel(count, width, extra, *refs):
    base, near, near_rows, far, far_rows = refs[:5]
    outs = refs[6:] if extra else refs[5:]
    rows = outs[0].shape[1]
    slots = near.shape[1] // count
    for j in range(count):
        part = slice(j * slots, (j + 1) * slots)
        own = slice(j * rows, (j + 1) * rows)
        total = base[0, own, :].astype(F32)
        total = total + dot_tn(near[0, part, :], near_rows[0, part, :])
        total = total + dot_tn(far[0, part, :], far_rows[0, part, :])
        outs[j][0, :, :width] = total.astype(BF16)
        if extra:
            outs[j][0, :, width:] = refs[5][0, own, :]


def spread_blocks(base, side, near, near_rows, far, far_rows, columns=None):
    seqs, total, piece = near.shape
    width = base.shape[2]
    count = base.shape[1] // (2 * piece)
    group = count * piece
    first = lambda s: (s, 0, 0)
    table = pl.BlockSpec((1, total, piece), first)
    slot_rows = pl.BlockSpec((1, total, width), first)
    specs = [
        pl.BlockSpec((1, group, width), lambda s: (s, side, 0)),
        table,
        slot_rows,
        table,
        slot_rows,
    ]
    operands = [base, near, near_rows, far, far_rows]
    out_width = width
    if columns is not None:
        specs.append(pl.BlockSpec((1, group, columns.shape[2]), first))
        operands.append(columns)
        out_width = width + columns.shape[2]
    return pl.pallas_call(
        functools.partial(spread_kernel, count, width, columns is not None),
        grid=(seqs,),
        in_specs=specs,
        out_specs=[pl.BlockSpec((1, piece, out_width), first)] * count,
        out_shape=[jax.ShapeDtypeStruct((seqs, piece, out_width), BF16)] * count,
        cost_estimate=pl.CostEstimate(
            flops=4 * seqs * total * piece * width,
            transcendentals=0,
            bytes_accessed=4 * seqs * (group + total) * width,
        ),
        name="spread",
    )(*operands)


def after(value, *others):
    return lax.optimization_barrier((value, *others))[0]


def shards(
    hidden_in,
    out_grad,
    routes,
    block_order,
    norm_attn,
    w_query,
    w_kv_down,
    norm_latent,
    w_key_up,
    w_value_up,
    w_out,
    norm_ffn,
    w_router,
    shared_gate,
    shared_up,
    shared_down,
    expert_gate,
    expert_up,
    expert_down,
):
    seqs, piece, width = hidden_in.shape
    n_expert = lax.axis_size("expert")
    n_ctx = lax.axis_size("ctx")
    n_dp = lax.axis_size("dp")
    lanes = n_expert // 2
    heads = w_query.shape[1] // (NOPE + ROPE)
    expert_count = w_router.shape[1]
    slots = 8 * ((piece * TOP + 6 * expert_count - 1) // (6 * expert_count))
    expert_rank = lax.axis_index("expert")
    ctx_rank = lax.axis_index("ctx")
    dp_rank = lax.axis_index("dp")
    span = piece * n_expert
    total_rows = span * n_ctx
    scale = (NOPE + ROPE) ** (-0.5)
    group = lanes * piece
    group_slots = lanes * slots

    def shift(value, steps):
        pairs = [(e, (e + 2 * steps) % n_expert) for e in range(n_expert)]
        return lax.ppermute(value, "expert", pairs)

    def across(value):
        return lax.ppermute(value, "expert", [(e, e ^ 1) for e in range(n_expert)])

    def other_dp(value):
        return lax.ppermute(value, "dp", [(d, n_dp - 1 - d) for d in range(n_dp)])

    def other_ctx(value):
        return lax.ppermute(value, "ctx", [(c, n_ctx - 1 - c) for c in range(n_ctx)])

    up_count = lanes // 2
    down_count = lanes - 1 - up_count

    def gather_blocks(own):
        other = [across(own)]
        ups, downs = [own], [own]
        for k in range(max(up_count, down_count)):
            if k < up_count:
                ups.append(shift(ups[-1], 1))
            if k < down_count:
                downs.append(shift(downs[-1], -1))
        column = ups + downs[:0:-1]
        return column + other + [across(b) for b in column[1:]]

    def gather_ctx(value):
        if n_ctx == 2:
            return jnp.concatenate([value, other_ctx(value)], axis=1), [ctx_rank, 1 - ctx_rank]
        return lax.all_gather(value, "ctx", axis=1, tiled=True), list(range(n_ctx))

    def scatter_ctx(value):
        if n_ctx == 2:
            half = value.shape[1] // 2
            return add(value[:, :half], other_ctx(value[:, half:]))
        return lax.psum_scatter(value, "ctx", scatter_dimension=1, tiled=True)

    def add(*terms):
        total = terms[0].astype(F32)
        for term in terms[1:]:
            total = total + term.astype(F32)
        return total.astype(BF16)

    def scatter_blocks(part):
        order = [up_count] + [k for k in range(lanes - 1, 0, -1) if k != up_count] + [0]
        crossed = {k: across(part(lanes + k)) for k in order}
        sums = {k: (part(k), crossed[k]) for k in order}
        moving = add(*sums[up_count])
        for k in range(up_count, 0, -1):
            moving = shift(moving, -1)
            if k > 1:
                moving = add(*sums[k - 1], moving)
        result = [*sums[0], moving]
        if down_count:
            moving = add(*sums[lanes - down_count])
            for d in range(down_count, 0, -1):
                moving = shift(moving, 1)
                if d > 1:
                    moving = add(*sums[lanes - d + 1], moving)
            result.append(moving)
        return sum(term.astype(F32) for term in result)

    def sum_copies(grad):
        sent = grad.astype(BF16)
        if n_ctx != 2:
            return lax.psum(sent, ("dp", "ctx")).astype(F32)
        half = grad.shape[0] // 2
        mine = lax.dynamic_slice_in_dim(sent, ctx_rank * half, half, 0)
        theirs = lax.dynamic_slice_in_dim(sent, (1 - ctx_rank) * half, half, 0)
        pair = add(mine, other_ctx(theirs))
        full = add(pair, other_dp(pair))
        rest = other_ctx(full)
        first = ctx_rank == 0
        return jnp.concatenate(
            [jnp.where(first, full, rest), jnp.where(first, rest, full)], axis=0
        ).astype(F32)

    def split_copies(grad):
        sent = grad.astype(BF16)
        if n_ctx != 2:
            return lax.psum_scatter(sent, "ctx", scatter_dimension=0, tiled=True).astype(F32)
        half = grad.shape[0] // 2
        theirs = lax.dynamic_slice_in_dim(sent, (1 - ctx_rank) * half, half, 0)
        mine = lax.dynamic_slice_in_dim(sent, ctx_rank * half, half, 0)
        return mine.astype(F32) + other_ctx(theirs).astype(F32)

    rank_z, rank_x = expert_rank // 2, expert_rank % 2
    owners = [
        ((rank_z - j % lanes) % lanes) * 2 + (rank_x + j // lanes) % 2 for j in range(n_expert)
    ]
    owner_ids = jnp.stack(owners)
    ids = jnp.arange(n_expert, dtype=jnp.int32)
    block_of = ((ids % 2 + rank_x) % 2) * lanes + (rank_z - ids // 2) % lanes

    kv_rows = w_kv_down.shape[0]
    kv_piece = kv_rows // n_ctx
    kv_own = lax.dynamic_slice_in_dim(w_kv_down, ctx_rank * kv_piece, kv_piece, 0)
    kv_span = join([b[None] for b in gather_blocks(kv_own)])
    kv_all, kv_ranks = gather_ctx(kv_span)
    kv_ranks = jnp.stack([jnp.asarray(r, jnp.int32) for r in kv_ranks])
    place_of = jnp.zeros((n_ctx,), jnp.int32)
    for i in range(n_ctx):
        place_of = jnp.where(jnp.arange(n_ctx) == kv_ranks[i], i, place_of)
    kv_index = (place_of[None, :] * n_expert + block_of[:, None]).reshape(-1)
    kv_full = reorder(kv_all, kv_index)[0]

    blocks = gather_blocks(hidden_in)

    def rms(rows):
        return lax.rsqrt(jnp.mean(rows * rows, axis=-1, keepdims=True) + EPSILON)

    half_rows = total_rows // (2 * n_ctx)

    def positions(row_ids):
        matches = (row_ids // half_rows)[:, None] == jnp.arange(2 * n_ctx, dtype=jnp.int32)
        starts = jnp.sum(jnp.where(matches[None], block_order[:, None, :], 0), axis=2)
        return starts * half_rows + row_ids % half_rows

    piece_ids = jnp.arange(piece, dtype=jnp.int32)
    in_span = (owner_ids[:, None] * piece + piece_ids[None, :]).reshape(-1)
    span_pos = positions(ctx_rank * span + in_span)
    key_pos = positions((kv_ranks[:, None] * span + in_span[None, :]).reshape(-1))
    own_tables = rope_tables(span_pos[:, :piece])
    span_cos, span_sin = rope_tables(span_pos)
    turns = jnp.concatenate([span_cos, span_cos, span_sin, span_sin], axis=-1)
    span_cos = jnp.tile(span_cos, (1, 1, 2 * heads))
    span_sin = jnp.tile(span_sin, (1, 1, 2 * heads))

    own_rows = hidden_in.astype(F32)
    inv_own = rms(own_rows)
    unit_own = own_rows * inv_own
    normed_own = (unit_own * norm_attn).astype(BF16)
    kv_joint = product(normed_own, kv_full)
    latent_raw = kv_joint[..., :LATENT]
    inv_latent = rms(latent_raw)
    unit_latent = latent_raw * inv_latent
    latent_own = jnp.concatenate(
        [
            unit_latent * norm_latent,
            rotate(kv_joint[..., LATENT:], own_tables),
            routes.astype(F32),
            jnp.zeros((seqs, piece, ROPE - TOP), F32),
        ],
        axis=-1,
    ).astype(BF16)
    latent_span = join(gather_blocks(latent_own))
    latent_all, _ = gather_ctx(latent_span)
    grad_all = lax.all_gather(after(out_grad, blocks[2]), "expert", axis=1, tiled=True)

    per_head = w_query.reshape(width, heads, NOPE + ROPE)
    w_nope = per_head[..., :NOPE].reshape(width, heads * NOPE)
    w_rope = per_head[..., NOPE:]
    first, second = halves(w_rope)
    w_turned = jnp.concatenate([-second, first], axis=-1).reshape(width, heads * ROPE)
    w_inner = jnp.concatenate(
        [w_nope, w_rope.reshape(width, heads * ROPE), w_turned], axis=-1
    )
    normed_span = join(blocks, norm_attn)
    query_raw = product(normed_span, w_inner)
    flat = heads * NOPE
    queries = jnp.concatenate(
        [
            query_raw[..., :flat],
            query_raw[..., flat : flat + heads * ROPE] * span_cos
            + query_raw[..., flat + heads * ROPE :] * span_sin,
        ],
        axis=-1,
    ).astype(BF16)
    latent_part = latent_all[..., :LATENT]
    key_rope = latent_all[..., LATENT : LATENT + ROPE]
    rope_first, rope_second = halves(key_rope)
    key_rope = jnp.concatenate([key_rope, rope_second, -rope_first], axis=-1)
    w_up = jnp.concatenate([w_key_up, w_value_up], axis=-1)
    pairs = product(latent_part, w_up).astype(BF16)
    heads_out, lse = attend(queries, pairs, key_rope, span_pos, key_pos, heads, scale)

    def block_of_span(array, j):
        return array[:, j * piece : (j + 1) * piece]

    attn_own = scatter_blocks(
        lambda j: product(block_of_span(heads_out, j), w_out).astype(BF16)
    )
    residual = own_rows + attn_own
    inv_ffn = rms(residual)
    unit_ffn = residual * inv_ffn
    normed_ffn = (unit_ffn * norm_ffn).astype(BF16)

    routes_span = (
        latent_span[..., LATENT + ROPE : LATENT + ROPE + TOP]
        .astype(jnp.int32)
        .reshape(seqs, n_expert, piece, TOP)
    )
    mine = dp_rank * n_expert + expert_rank
    theirs = (n_dp - 1 - dp_rank) * n_expert + expert_rank
    earlier = (piece_ids[:, None] < piece_ids[None, :]).astype(F32)
    slot_ids = jnp.arange(slots, dtype=jnp.int32)
    hits, picks = [], []
    for target in (mine, theirs):
        hit = routes_span == target
        named = jnp.any(hit, axis=-1)
        rank = jnp.einsum("sjp,pq->sjq", named.astype(F32), earlier).astype(jnp.int32)
        hits.append(hit)
        picks.append(jnp.where(named, rank, -1)[:, :, None, :] == slot_ids[:, None])
    picks_bf = [pick.astype(BF16) for pick in picks]

    def side_tables(table):
        return [
            table[:, side * lanes : (side + 1) * lanes].reshape(seqs, group_slots, piece)
            for side in range(2)
        ]

    near_tables, far_tables = side_tables(picks_bf[0]), side_tables(picks_bf[1])
    grad_span = reorder(grad_all, owner_ids)

    def span_blocks(array, side):
        return [block_of_span(array, side * lanes + k) for k in range(lanes)]

    grad_slots = [
        pick_blocks(span_blocks(grad_span, side), near_tables[side], far_tables[side])
        for side in range(2)
    ]
    grad_got = [other_dp(grad_slots[side][1]) for side in range(2)]

    sh_dhidden = back_product(grad_span, shared_down)
    ffn_blocks = gather_blocks(after(normed_ffn, sh_dhidden, *[g[1] for g in grad_slots]))
    token_slots = [
        pick_blocks(
            ffn_blocks[side * lanes : (side + 1) * lanes], near_tables[side], far_tables[side]
        )
        for side in range(2)
    ]
    token_got = [other_dp(token_slots[side][1]) for side in range(2)]
    ffn_span = join([after(b, token_slots[1][1]) for b in ffn_blocks])
    logits_span = product(ffn_span, w_router)
    routes_flat = routes_span.reshape(seqs, span, TOP)
    hot_span = routes_flat[..., None] == jnp.arange(expert_count, dtype=jnp.int32)
    chosen_span = jnp.sum(jnp.where(hot_span, logits_span[:, :, None, :], 0.0), axis=-1)
    gates_span = jax.nn.softmax(chosen_span, axis=-1).reshape(seqs, n_expert, piece, TOP)
    gated = [
        jnp.where(
            pick, jnp.sum(jnp.where(hit, gates_span, 0.0), axis=-1)[:, :, None, :], 0.0
        )
        for hit, pick in zip(hits, picks)
    ]
    slot_gates = [
        jnp.sum(weights, axis=-1).reshape(seqs, 2, group_slots).transpose(1, 0, 2)
        for weights in gated
    ]
    gates_got = other_dp(slot_gates[1])

    sh_gate = product(ffn_span, shared_gate)
    sh_up = product(ffn_span, shared_up)
    sh_hidden = (jax.nn.silu(sh_gate) * sh_up).astype(BF16)
    sh_dgate, sh_dup = silu_grads(sh_dhidden, sh_gate, sh_up)
    sh_dnorm = (back_product(sh_dgate, shared_gate) + back_product(sh_dup, shared_up)).astype(BF16)

    half_slots = 2 * seqs * group_slots

    def expert(tokens, grads, gates):
        rows_in = jnp.stack(tokens).reshape(half_slots, width)
        raw = jnp.stack(grads).reshape(half_slots, width)
        grads_in = (raw.astype(F32) * gates.reshape(half_slots, 1)).astype(BF16)
        ex_gate = product(rows_in, expert_gate[0])
        ex_up = product(rows_in, expert_up[0])
        ex_hidden = (jax.nn.silu(ex_gate) * ex_up).astype(BF16)
        ex_dgate, ex_dup = silu_grads(back_product(grads_in, expert_down[0]), ex_gate, ex_up)
        ex_dx = (
            back_product(ex_dgate, expert_gate[0]) + back_product(ex_dup, expert_up[0])
        ).astype(BF16)
        ex_out = product(ex_hidden, expert_down[0]).astype(BF16)
        dg = jnp.sum(raw.astype(F32) * ex_out.astype(F32), axis=-1)
        return rows_in, grads_in, ex_hidden, ex_dgate, ex_dup, ex_dx, ex_out, dg

    shape = (2, seqs, group_slots)
    far = expert([after(t, sh_dnorm) for t in token_got], grad_got, gates_got)
    far_dx = far[5].reshape(shape + (width,))
    dx_back = [None, None]
    dx_back[1] = other_dp(far_dx[1])
    dx_back[0] = other_dp(far_dx[0])
    dg_back = other_dp(far[7].reshape(shape))
    out_back = other_dp(after(far[6], *dx_back).reshape(shape + (width,)))
    near = expert(
        [after(t[0], far[5]) for t in token_slots], [g[0] for g in grad_slots], slot_gates[0]
    )
    near_dx = near[5].reshape(shape + (width,))
    near_dg = near[7].reshape(shape)

    lane_ids = jnp.arange(128, dtype=jnp.int32)

    def dg_columns(side):
        columns = 0.0
        for pick, dg, target in ((picks[0], near_dg, mine), (picks[1], dg_back, theirs)):
            table = pick[:, side * lanes : (side + 1) * lanes]
            values = dg[side].reshape(seqs, lanes, slots, 1)
            rows = jnp.sum(jnp.where(table, values, 0.0), axis=2).reshape(seqs, group, 1)
            top = rows.astype(BF16).astype(F32)
            columns = columns + jnp.where(lane_ids == target, top, 0.0)
            columns = columns + jnp.where(lane_ids == target + expert_count, rows - top, 0.0)
        return columns.astype(BF16)

    dnorm_blocks = [
        spread_blocks(
            sh_dnorm,
            side,
            near_tables[side],
            near_dx[side],
            far_tables[side],
            dx_back[side],
            dg_columns(side),
        )
        for side in range(2)
    ]
    dnorm_sum = scatter_blocks(lambda j: dnorm_blocks[j // lanes][j % lanes])
    dg_own = (
        dnorm_sum[..., width : width + expert_count]
        + dnorm_sum[..., width + expert_count : width + 2 * expert_count]
    )
    dnorm_sum = dnorm_sum[..., :width]
    route_hot = routes[..., None] == jnp.arange(expert_count, dtype=jnp.int32)
    logits = product(normed_ffn, w_router)
    chosen = jnp.sum(jnp.where(route_hot, logits[:, :, None, :], 0.0), axis=-1)
    gate_weights = jax.nn.softmax(chosen, axis=-1)
    grad_choice = jnp.sum(jnp.where(route_hot, dg_own[:, :, None, :], 0.0), axis=-1)
    grad_chosen = gate_weights * (
        grad_choice - jnp.sum(gate_weights * grad_choice, axis=-1, keepdims=True)
    )
    grad_logits = jnp.sum(jnp.where(route_hot, grad_chosen[..., None], 0.0), axis=2).astype(BF16)
    dnorm_ffn = dnorm_sum + back_product(grad_logits, w_router)
    grad_router = weight_grad(normed_ffn, grad_logits)
    grad_gain_ffn = jnp.sum(dnorm_ffn * unit_ffn, axis=(0, 1))
    grad_resid = out_grad.astype(F32) + norm_back(dnorm_ffn, residual, inv_ffn, norm_ffn)

    sh_out = product(after(sh_hidden, dnorm_blocks[0][0]), shared_down).astype(BF16)
    near_out = near[6].reshape(shape + (width,))
    out_blocks = []
    for side, (near_gates, far_gates) in enumerate(
        zip(*[side_tables(weights.astype(BF16)) for weights in gated])
    ):
        out_blocks += spread_blocks(
            sh_out, side, near_gates, near_out[side], far_gates, out_back[side]
        )
    out_part = reorder(join(out_blocks), block_of)
    out_own = lax.psum_scatter(out_part, "expert", scatter_dimension=1, tiled=True)
    out_hidden = (residual + out_own.astype(F32)).astype(BF16)

    grad_attn = join(gather_blocks(grad_resid.astype(BF16)))

    both = [
        after(jnp.concatenate(pair, axis=0), dnorm_blocks[0][0]) for pair in zip(far[:5], near[:5])
    ]
    rows_in, grads_in, ex_hidden, ex_dgate, ex_dup = both
    exp_grads = (
        split_copies(weight_grad(rows_in, ex_dgate))[None],
        split_copies(weight_grad(rows_in, ex_dup))[None],
        split_copies(weight_grad(ex_hidden, grads_in))[None],
    )
    grad_sh_in = sum_copies(
        after(
            weight_grad(
                ffn_span,
                after(jnp.concatenate([sh_dgate, sh_dup], axis=-1), dnorm_blocks[0][0]),
            ).astype(BF16),
            out_back,
        )
    )
    grad_sh_down = sum_copies(
        after(
            weight_grad(after(sh_hidden, dnorm_blocks[0][0]), grad_span).astype(BF16), out_back
        )
    )
    shared_width = shared_gate.shape[1]

    grad_heads = back_product(grad_attn, w_out).astype(BF16)
    grad_out_w = sum_copies(weight_grad(heads_out, grad_attn))
    grad_queries, grad_pairs, grad_key_rope = attend_back(
        queries, pairs, key_rope, grad_heads, lse, span_pos, key_pos, turns, heads, scale
    )
    grad_latent = jnp.concatenate(
        [back_product(grad_pairs, w_up).astype(BF16), grad_key_rope], axis=-1
    )

    def by_rank(array):
        return array.reshape(n_expert, -1)

    def padded(array, size):
        return jnp.pad(array, ((0, 0), (0, size - array.shape[1])))

    room = seqs * piece * ROPE
    early = jnp.concatenate([by_rank(grad_gain_ffn), by_rank(grad_router)], axis=1)
    early_size = early.shape[1]
    early = jnp.take(padded(early, room).astype(BF16), owner_ids, axis=0, mode="clip")
    early = early.reshape(n_expert, seqs, piece, ROPE).transpose(1, 0, 2, 3)
    grad_latent_span = jnp.concatenate(
        [scatter_ctx(grad_latent), early.reshape(seqs, span, ROPE)], axis=-1
    )
    grad_latent_own = scatter_blocks(lambda j: block_of_span(grad_latent_span, j))
    early = grad_latent_own[..., LATENT + ROPE :].reshape(-1)[:early_size]
    dnorm_own = scatter_blocks(
        lambda j: back_product(block_of_span(grad_queries, j), w_query).astype(BF16)
    )
    grad_query_part = weight_grad(normed_span, grad_queries)
    grad_up_part = weight_grad(latent_part, grad_pairs)
    grad_query_w = sum_copies(grad_query_part)
    grad_up = sum_copies(grad_up_part)

    gain_part = jnp.sum(grad_query_part * w_query.astype(F32), axis=-1) / norm_attn
    gain_latent_part = jnp.sum(grad_up_part * w_up.astype(F32), axis=-1) / norm_latent
    late = jnp.concatenate([by_rank(gain_part), by_rank(gain_latent_part)], axis=1)
    late_size = late.shape[1]
    late = padded(late.reshape(1, -1), room).astype(BF16).reshape(seqs, piece, ROPE)

    grad_unit = grad_latent_own[..., :LATENT]
    grad_kv = jnp.concatenate(
        [
            norm_back(grad_unit, latent_raw, inv_latent, norm_latent),
            unrotate(grad_latent_own[..., LATENT : LATENT + ROPE], own_tables),
        ],
        axis=-1,
    ).astype(BF16)
    dnorm_kv = back_product(grad_kv, kv_full)
    in_grad = (
        grad_resid + norm_back(dnorm_own + dnorm_kv, own_rows, inv_own, norm_attn)
    ).astype(BF16)
    grad_kv_span = join(gather_blocks(jnp.concatenate([grad_kv, late], axis=-1)))
    normed_cols = lax.dynamic_slice_in_dim(normed_span, expert_rank * kv_rows, kv_rows, 2)
    late = (
        grad_kv_span[..., LATENT + ROPE :]
        .reshape(seqs, n_expert, piece, ROPE)
        .transpose(1, 0, 2, 3)
        .reshape(n_expert, -1)[:, : n_expert * late_size]
        .reshape(n_expert, n_expert, late_size)
    )
    late = jnp.sum(
        lax.dynamic_index_in_dim(late, expert_rank, 1, False).astype(F32), axis=0
    )
    rows = width // n_expert
    small = padded(jnp.concatenate([late, early])[None], kv_rows * ROPE).reshape(kv_rows, ROPE)
    kv_small = sum_copies(
        jnp.concatenate(
            [weight_grad(normed_cols, grad_kv_span[..., : LATENT + ROPE]), small], axis=-1
        )
    )
    grad_kv_w = kv_small[:, : LATENT + ROPE]
    small = kv_small[:, LATENT + ROPE :].reshape(-1)
    late, early = small[:late_size], small[late_size : late_size + early_size]
    own_gain = lax.dynamic_slice_in_dim(norm_attn, expert_rank * rows, rows, 0)
    gain_kv = jnp.sum(grad_kv_w * w_kv_down.astype(F32), axis=-1) / own_gain
    return (
        out_hidden,
        in_grad,
        late[:rows] + gain_kv,
        grad_query_w,
        grad_kv_w,
        late[rows:],
        grad_up[:, :flat],
        grad_up[:, flat:],
        grad_out_w,
        early[:rows],
        early[rows:].reshape(rows, expert_count),
        grad_sh_in[:, :shared_width],
        grad_sh_in[:, shared_width:],
        grad_sh_down,
        exp_grads[0],
        exp_grads[1],
        exp_grads[2],
    )


def solution(mesh):
    return jax.shard_map(
        shards,
        mesh=mesh,
        in_specs=(
            P("dp", ("ctx", "expert"), None),
            P("dp", ("ctx", "expert"), None),
            P("dp", ("ctx", "expert"), None),
            P("dp", None),
            P(),
            P(None, "expert"),
            P("expert", None),
            P(),
            P(None, "expert"),
            P(None, "expert"),
            P("expert", None),
            P(),
            P(),
            P(None, "expert"),
            P(None, "expert"),
            P("expert", None),
            P(("dp", "expert"), None, None),
            P(("dp", "expert"), None, None),
            P(("dp", "expert"), None, None),
        ),
        out_specs=(
            P("dp", ("ctx", "expert"), None),
            P("dp", ("ctx", "expert"), None),
            P("expert"),
            P(None, "expert"),
            P("expert", None),
            P("expert"),
            P(None, "expert"),
            P(None, "expert"),
            P("expert", None),
            P("expert"),
            P("expert", None),
            P(None, "expert"),
            P(None, "expert"),
            P("expert", None),
            P(("dp", "expert"), "ctx", None),
            P(("dp", "expert"), "ctx", None),
            P(("dp", "expert"), "ctx", None),
        ),
        check_vma=False,
    )
```

```python
import functools

import jax
import jax.numpy as jnp
from jax import lax
from jax.experimental import pallas as pl
from jax.experimental.pallas import tpu as pltpu
from jax.sharding import PartitionSpec as P


NOPE = 128
ROPE = 64
VDIM = 128
LATENT = 512
TOP = 6
EPSILON = 1e-06
MASKED = -1e30
BF16 = jnp.bfloat16
F32 = jnp.float32
EXPERT, CTX, DP = "expert", "ctx", "dp"


def product(inputs, matrix):
    return jnp.dot(inputs, matrix, preferred_element_type=F32)


def back_product(gradient, matrix):
    return lax.dot_general(
        gradient,
        matrix,
        (((gradient.ndim - 1,), (1,)), ((), ())),
        preferred_element_type=F32,
    )


def weight_grad(inputs, gradient):
    flat_in = inputs.reshape(-1, inputs.shape[-1])
    flat_grad = gradient.reshape(-1, gradient.shape[-1])
    return lax.dot_general(
        flat_in, flat_grad, (((0,), (0,)), ((), ())), preferred_element_type=F32
    )


def rope_tables(positions):
    inverse = 10000.0 ** (-2.0 * jnp.arange(ROPE // 2, dtype=F32) / ROPE)
    angles = positions.astype(F32)[..., None] * inverse
    return jnp.cos(angles), jnp.sin(angles)


def halves(vectors):
    return vectors[..., : ROPE // 2], vectors[..., ROPE // 2 :]


def rotate(vectors, tables):
    first, second = halves(vectors)
    cosine, sine = tables
    return jnp.concatenate(
        [first * cosine - second * sine, second * cosine + first * sine], axis=-1
    )


def unrotate(gradient, tables):
    first, second = halves(gradient)
    cosine, sine = tables
    return jnp.concatenate(
        [first * cosine + second * sine, second * cosine - first * sine], axis=-1
    )


def norm_back(gradient, inputs, inverse_rms, gain_vec):
    scaled = gradient * gain_vec
    return inverse_rms * scaled - inputs * inverse_rms**3 * jnp.mean(
        inputs * scaled, axis=-1, keepdims=True
    )


def silu_grads(grad_hidden, gate, upward):
    sigmoid_gate = jax.nn.sigmoid(gate)
    grad_gate = grad_hidden * upward * sigmoid_gate * (1.0 + gate * (1.0 - sigmoid_gate))
    grad_upward = grad_hidden * gate * sigmoid_gate
    return (grad_gate.astype(BF16), grad_upward.astype(BF16))


def dot_nt(left, right):
    return lax.dot_general(left, right, (((1,), (1,)), ((), ())), preferred_element_type=F32)


def dot_tn(left, right):
    return lax.dot_general(left, right, (((0,), (0,)), ((), ())), preferred_element_type=F32)


def dot_nn(left, right):
    return lax.dot_general(left, right, (((1,), (0,)), ((), ())), preferred_element_type=F32)


def head_cols(head):
    return slice(head * NOPE, (head + 1) * NOPE)


def rope_cols(heads, head):
    start = heads * NOPE + head * ROPE
    return slice(start, start + ROPE)


def forward_kernel(heads, scale, q_ref, k_ref, v_ref, kr_ref, pq_ref, pk_ref, o_ref, lse_ref):
    allowed = pk_ref[0] <= pq_ref[0]
    for head in range(heads):
        cols = head_cols(head)
        scores = dot_nt(k_ref[0, :, cols], q_ref[0, :, cols])
        scores = scores + dot_nt(kr_ref[0, :, :ROPE], q_ref[0, :, rope_cols(heads, head)])
        scores = jnp.where(allowed, scores * scale, MASKED)
        top = jnp.max(scores, axis=0, keepdims=True)
        weights = jnp.exp(scores - top)
        total = jnp.sum(weights, axis=0, keepdims=True)
        lse_ref[0, head : head + 1, :] = top + jnp.log(total)
        probs = (weights * (1.0 / total)).astype(BF16)
        o_ref[0, :, cols] = dot_tn(probs, v_ref[0, :, cols]).astype(BF16)


def backward_kernel(
    heads,
    scale,
    q_ref,
    k_ref,
    v_ref,
    kr_ref,
    do_ref,
    lse_ref,
    pq_ref,
    pk_ref,
    turn_ref,
    dq_ref,
    dkv_ref,
    dkr_ref,
    dkv_acc,
    dkr_acc,
):
    step = pl.program_id(1)

    @pl.when(step == 0)
    def _():
        dkv_acc[...] = jnp.zeros_like(dkv_acc)
        dkr_acc[...] = jnp.zeros_like(dkr_acc)

    allowed = pk_ref[0] <= pq_ref[0]
    pieces = []
    for head in range(heads):
        cols = head_cols(head)
        value_cols = head_cols(heads + head)
        keys = k_ref[0, :, cols]
        query = q_ref[0, :, cols]
        query_rope = q_ref[0, :, rope_cols(heads, head)]
        grad = do_ref[0, :, cols]
        scores = dot_nt(keys, query) + dot_nt(kr_ref[0, :, :ROPE], query_rope)
        probs = jnp.where(
            allowed, jnp.exp(scores * scale - lse_ref[0, head : head + 1, :]), 0.0
        )
        grad_probs = dot_nt(v_ref[0, :, cols], grad)
        inner = jnp.sum(probs * grad_probs, axis=0, keepdims=True)
        grad_raw = (probs * (grad_probs - inner) * scale).astype(BF16)
        dkv_acc[:, value_cols] += dot_nn(probs.astype(BF16), grad)
        dkv_acc[:, cols] += dot_nn(grad_raw, query)
        dkr_acc[...] += dot_nn(grad_raw, query_rope)
        turned = dot_tn(grad_raw, kr_ref[0]) * turn_ref[0]
        pieces.append(dot_tn(grad_raw, keys))
        pieces.append(turned[:, :ROPE] + turned[:, ROPE:])
    dq_ref[0] = jnp.concatenate(pieces, axis=1).astype(BF16)

    @pl.when(step == pl.num_programs(1) - 1)
    def _():
        dkv_ref[0] = dkv_acc[...].astype(BF16)
        dkr_ref[0] = dkr_acc[...].astype(BF16)


def query_tile(rows, total_rows):
    return min(rows, max(128, 256 * 1024 // total_rows))


def attend(queries, pairs, key_rope, pos_q, pos_k, heads, scale):
    seqs, rows, width = queries.shape
    total_rows = pairs.shape[1]
    tile = query_tile(rows, total_rows)
    flat = heads * NOPE
    return pl.pallas_call(
        functools.partial(forward_kernel, heads, scale),
        grid=(seqs, rows // tile),
        in_specs=[
            pl.BlockSpec((1, tile, width), lambda s, i: (s, i, 0)),
            pl.BlockSpec((1, total_rows, flat), lambda s, i: (s, 0, 0)),
            pl.BlockSpec((1, total_rows, flat), lambda s, i: (s, 0, 1)),
            pl.BlockSpec((1, total_rows, 2 * ROPE), lambda s, i: (s, 0, LATENT // (2 * ROPE))),
            pl.BlockSpec((1, 1, tile), lambda s, i: (s, 0, i)),
            pl.BlockSpec((1, total_rows, 1), lambda s, i: (s, 0, 0)),
        ],
        out_specs=[
            pl.BlockSpec((1, tile, flat), lambda s, i: (s, i, 0)),
            pl.BlockSpec((1, heads, tile), lambda s, i: (s, 0, i)),
        ],
        out_shape=[
            jax.ShapeDtypeStruct((seqs, rows, flat), BF16),
            jax.ShapeDtypeStruct((seqs, heads, rows), F32),
        ],
        cost_estimate=pl.CostEstimate(
            flops=2 * seqs * heads * rows * total_rows * (NOPE + ROPE + VDIM),
            transcendentals=seqs * heads * rows * total_rows,
            bytes_accessed=2 * seqs * (rows * width + 2 * total_rows * flat),
        ),
    )(queries, pairs, pairs, key_rope, pos_q[:, None, :], pos_k[:, :, None])


def attend_back(queries, pairs, key_rope, grads, lse, pos_q, pos_k, turns, heads, scale):
    seqs, rows, width = queries.shape
    total_rows = pairs.shape[1]
    tile = query_tile(rows, total_rows)
    flat = heads * NOPE
    whole = lambda s, i: (s, 0, 0)
    piece = lambda s, i: (s, i, 0)
    return pl.pallas_call(
        functools.partial(backward_kernel, heads, scale),
        grid=(seqs, rows // tile),
        in_specs=[
            pl.BlockSpec((1, tile, width), piece),
            pl.BlockSpec((1, total_rows, flat), whole),
            pl.BlockSpec((1, total_rows, flat), lambda s, i: (s, 0, 1)),
            pl.BlockSpec((1, total_rows, 2 * ROPE), lambda s, i: (s, 0, LATENT // (2 * ROPE))),
            pl.BlockSpec((1, tile, flat), piece),
            pl.BlockSpec((1, heads, tile), lambda s, i: (s, 0, i)),
            pl.BlockSpec((1, 1, tile), lambda s, i: (s, 0, i)),
            pl.BlockSpec((1, total_rows, 1), whole),
            pl.BlockSpec((1, tile, 2 * ROPE), piece),
        ],
        out_specs=[
            pl.BlockSpec((1, tile, width), piece),
            pl.BlockSpec((1, total_rows, 2 * flat), whole),
            pl.BlockSpec((1, total_rows, ROPE), whole),
        ],
        out_shape=[
            jax.ShapeDtypeStruct((seqs, rows, width), BF16),
            jax.ShapeDtypeStruct((seqs, total_rows, 2 * flat), BF16),
            jax.ShapeDtypeStruct((seqs, total_rows, ROPE), BF16),
        ],
        scratch_shapes=[
            pltpu.VMEM((total_rows, 2 * flat), F32),
            pltpu.VMEM((total_rows, ROPE), F32),
        ],
        cost_estimate=pl.CostEstimate(
            flops=4 * seqs * heads * rows * total_rows * (NOPE + ROPE + VDIM),
            transcendentals=seqs * heads * rows * total_rows,
            bytes_accessed=2 * seqs * (rows * width + 4 * total_rows * flat),
        ),
    )(
        queries, pairs, pairs, key_rope, grads, lse, pos_q[:, None, :], pos_k[:, :, None], turns
    )


def join_kernel(count, *refs):
    rows = refs[0].shape[1]
    for j in range(count):
        refs[count][0, j * rows : (j + 1) * rows, :] = refs[j][0]


def join_norm_kernel(count, width, *refs):
    gain, out, tail = refs[count][...], refs[count + 1], refs[count + 2]
    rows = refs[0].shape[1]
    for j in range(count):
        values = refs[j][0, :, :width].astype(F32)
        inverse = lax.rsqrt(jnp.mean(values * values, axis=-1, keepdims=True) + EPSILON)
        part = slice(j * rows, (j + 1) * rows)
        out[0, part, :] = (values * inverse * gain).astype(BF16)
        tail[0, part, :] = refs[j][0, :, width:]


def join_norm(blocks, gain):
    seqs, rows, total = blocks[0].shape
    width = gain.shape[0]
    count = len(blocks)
    first = lambda s: (s, 0, 0)
    return pl.pallas_call(
        functools.partial(join_norm_kernel, count, width),
        grid=(seqs,),
        in_specs=[pl.BlockSpec((1, rows, total), first)] * count
        + [pl.BlockSpec((1, width), lambda s: (0, 0))],
        out_specs=[
            pl.BlockSpec((1, count * rows, width), first),
            pl.BlockSpec((1, count * rows, total - width), first),
        ],
        out_shape=[
            jax.ShapeDtypeStruct((seqs, count * rows, width), BF16),
            jax.ShapeDtypeStruct((seqs, count * rows, total - width), BF16),
        ],
        cost_estimate=pl.CostEstimate(
            flops=0, transcendentals=0, bytes_accessed=4 * seqs * count * rows * total
        ),
    )(*blocks, gain[None])


def join(blocks):
    seqs, rows, width = blocks[0].shape
    count = len(blocks)
    return pl.pallas_call(
        functools.partial(join_kernel, count),
        grid=(seqs,),
        in_specs=[pl.BlockSpec((1, rows, width), lambda s: (s, 0, 0))] * count,
        out_specs=pl.BlockSpec((1, count * rows, width), lambda s: (s, 0, 0)),
        out_shape=jax.ShapeDtypeStruct((seqs, count * rows, width), BF16),
        cost_estimate=pl.CostEstimate(
            flops=0, transcendentals=0, bytes_accessed=4 * seqs * count * rows * width
        ),
    )(*blocks)


def pick_kernel(count, slots, *refs):
    near, far = refs[count + 2], refs[count + 3]
    for j in range(count):
        rows = refs[j][0]
        part = slice(j * slots, (j + 1) * slots)
        near[0, part, :] = dot_nn(refs[count][0, part, :], rows).astype(BF16)
        far[0, part, :] = dot_nn(refs[count + 1][0, part, :], rows).astype(BF16)


def pick_blocks(blocks, near, far):
    seqs, rows, width = blocks[0].shape
    count = len(blocks)
    total = near.shape[1]
    block = pl.BlockSpec((1, rows, width), lambda s: (s, 0, 0))
    table = pl.BlockSpec((1, total, rows), lambda s: (s, 0, 0))
    out = pl.BlockSpec((1, total, width), lambda s: (s, 0, 0))
    return pl.pallas_call(
        functools.partial(pick_kernel, count, total // count),
        grid=(seqs,),
        in_specs=[block] * count + [table] * 2,
        out_specs=[out] * 2,
        out_shape=[jax.ShapeDtypeStruct((seqs, total, width), BF16)] * 2,
        cost_estimate=pl.CostEstimate(
            flops=4 * seqs * total * rows * width,
            transcendentals=0,
            bytes_accessed=2 * seqs * (count * rows + 2 * total) * width,
        ),
    )(*blocks, near, far)


def pick_span_kernel(count, slots, rows_ref, tail_ref, near_ref, far_ref, near, far):
    piece = rows_ref.shape[1] // count
    width = rows_ref.shape[2]
    for j in range(count):
        own = slice(j * piece, (j + 1) * piece)
        part = slice(j * slots, (j + 1) * slots)
        for table, out in ((near_ref, near), (far_ref, far)):
            picks = table[0, part, :]
            out[0, part, :width] = dot_nn(picks, rows_ref[0, own, :]).astype(BF16)
            out[0, part, width:] = dot_nn(picks, tail_ref[0, own, :]).astype(BF16)


def pick_span(span_rows, tail, side, near, far):
    seqs, total, piece = near.shape
    width, extra = span_rows.shape[2], tail.shape[2]
    count = span_rows.shape[1] // (2 * piece)
    half = lambda s: (s, side, 0)
    table = pl.BlockSpec((1, total, piece), lambda s: (s, 0, 0))
    out = pl.BlockSpec((1, total, width + extra), lambda s: (s, 0, 0))
    return pl.pallas_call(
        functools.partial(pick_span_kernel, count, total // count),
        grid=(seqs,),
        in_specs=[
            pl.BlockSpec((1, count * piece, width), half),
            pl.BlockSpec((1, count * piece, extra), half),
            table,
            table,
        ],
        out_specs=[out] * 2,
        out_shape=[jax.ShapeDtypeStruct((seqs, total, width + extra), BF16)] * 2,
        cost_estimate=pl.CostEstimate(
            flops=4 * seqs * total * piece * width,
            transcendentals=0,
            bytes_accessed=2 * seqs * (count * piece + 2 * total) * width,
        ),
    )(span_rows, tail, near, far)


def place_kernel(counts, dest_ref, *refs):
    out = refs[-1]
    p = 0
    for ref, count in zip(refs, counts):
        rows = ref.shape[1] // count
        for q in range(count):
            start = pl.multiple_of(dest_ref[p] * rows, rows)
            out[0, pl.ds(start, rows), :] = ref[0, q * rows : (q + 1) * rows, :]
            p += 1


def place(arrays, dest, rows):
    seqs, _, width = arrays[0].shape
    counts = [array.shape[1] // rows for array in arrays]
    total = rows * sum(counts)
    first = lambda s, dest: (s, 0, 0)
    return pl.pallas_call(
        functools.partial(place_kernel, counts),
        grid_spec=pltpu.PrefetchScalarGridSpec(
            num_scalar_prefetch=1,
            grid=(seqs,),
            in_specs=[pl.BlockSpec((1, array.shape[1], width), first) for array in arrays],
            out_specs=pl.BlockSpec((1, total, width), first),
        ),
        out_shape=jax.ShapeDtypeStruct((seqs, total, width), BF16),
        cost_estimate=pl.CostEstimate(
            flops=0, transcendentals=0, bytes_accessed=4 * seqs * total * width
        ),
    )(dest, *arrays)


def project_kernel(count, transposed, rows_ref, weight_ref, *outs):
    dot = dot_nt if transposed else dot_nn
    result = dot(rows_ref[0], weight_ref[...]).astype(BF16)
    piece = outs[0].shape[1]
    for j in range(count):
        outs[j][0] = result[j * piece : (j + 1) * piece]


def project(span_rows, side, weight, count, transposed):
    seqs, total, depth = span_rows.shape
    group = total // 2
    width = weight.shape[0] if transposed else weight.shape[1]
    return pl.pallas_call(
        functools.partial(project_kernel, count, transposed),
        grid=(seqs,),
        in_specs=[
            pl.BlockSpec((1, group, depth), lambda s: (s, side, 0)),
            pl.BlockSpec(weight.shape, lambda s: (0, 0)),
        ],
        out_specs=[pl.BlockSpec((1, group // count, width), lambda s: (s, 0, 0))] * count,
        out_shape=[jax.ShapeDtypeStruct((seqs, group // count, width), BF16)] * count,
        cost_estimate=pl.CostEstimate(
            flops=2 * seqs * group * depth * width,
            transcendentals=0,
            bytes_accessed=2 * (seqs * group * (depth + width) + depth * width),
        ),
    )(span_rows, weight)


def spread_kernel(count, width, extra, *refs):
    base, near, near_rows, far, far_rows = refs[:5]
    outs = refs[6:] if extra else refs[5:]
    rows = outs[0].shape[1]
    slots = near.shape[1] // count
    for j in range(count):
        part = slice(j * slots, (j + 1) * slots)
        own = slice(j * rows, (j + 1) * rows)
        total = base[0, own, :].astype(F32)
        total = total + dot_tn(near[0, part, :], near_rows[0, part, :])
        total = total + dot_tn(far[0, part, :], far_rows[0, part, :])
        outs[j][0, :, :width] = total.astype(BF16)
        if extra:
            outs[j][0, :, width:] = refs[5][0, own, :]


def spread_blocks(base, side, near, near_rows, far, far_rows, columns=None):
    seqs, total, piece = near.shape
    width = base.shape[2]
    count = base.shape[1] // (2 * piece)
    group = count * piece
    first = lambda s: (s, 0, 0)
    table = pl.BlockSpec((1, total, piece), first)
    slot_rows = pl.BlockSpec((1, total, width), first)
    specs = [
        pl.BlockSpec((1, group, width), lambda s: (s, side, 0)),
        table,
        slot_rows,
        table,
        slot_rows,
    ]
    operands = [base, near, near_rows, far, far_rows]
    out_width = width
    if columns is not None:
        specs.append(pl.BlockSpec((1, group, columns.shape[2]), first))
        operands.append(columns)
        out_width = width + columns.shape[2]
    return pl.pallas_call(
        functools.partial(spread_kernel, count, width, columns is not None),
        grid=(seqs,),
        in_specs=specs,
        out_specs=[pl.BlockSpec((1, piece, out_width), first)] * count,
        out_shape=[jax.ShapeDtypeStruct((seqs, piece, out_width), BF16)] * count,
        cost_estimate=pl.CostEstimate(
            flops=4 * seqs * total * piece * width,
            transcendentals=0,
            bytes_accessed=4 * seqs * (group + total) * width,
        ),
    )(*operands)


def expert_kernel(
    top_count,
    mine_ref,
    tok_a,
    tok_b,
    raw_a,
    raw_b,
    router,
    gate_hbm,
    up_hbm,
    down_hbm,
    x_out,
    dy_out,
    hid_out,
    dgate_out,
    dup_out,
    dx_a,
    dx_b,
    out_a,
    out_b,
    dg_out,
    w_gate,
    w_up,
    w_down,
    gates,
    sems,
):
    half, width = tok_a.shape
    hidden = w_gate.shape[1]
    tile = 256
    spans = [(f, min(tile, hidden - f)) for f in range(0, hidden, tile)]

    def copies(i, start, size):
        cols = pl.ds(start, size)
        return (
            pltpu.make_async_copy(gate_hbm.at[0, :, cols], w_gate.at[:, cols], sems.at[0, i]),
            pltpu.make_async_copy(up_hbm.at[0, :, cols], w_up.at[:, cols], sems.at[1, i]),
            pltpu.make_async_copy(down_hbm.at[0, cols, :], w_down.at[cols, :], sems.at[2, i]),
        )

    for i, (start, size) in enumerate(spans):
        for copy in copies(i, start, size):
            copy.start()
    mine = mine_ref[0].astype(F32)
    for part, (tok, raw) in enumerate(((tok_a, raw_a), (tok_b, raw_b))):
        rows = slice(part * half, (part + 1) * half)
        x_out[rows, :] = tok[...]
        logits = dot_nt(tok[...], router[...])
        experts = lax.broadcasted_iota(jnp.int32, logits.shape, 1).astype(F32)
        named = raw[:, width:].astype(F32)
        routes = [named[:, j : j + 1] for j in range(top_count)]
        chosen = [
            jnp.sum(jnp.where(experts == r, logits, 0.0), axis=-1, keepdims=True) for r in routes
        ]
        best = functools.reduce(jnp.maximum, chosen)
        powers = [jnp.exp(c - best) for c in chosen]
        wanted = sum(jnp.where(r == mine, p, 0.0) for r, p in zip(routes, powers))
        gate = wanted / sum(powers)
        gates[rows, :] = gate
        dy_out[rows, :] = (raw[:, :width].astype(F32) * gate).astype(BF16)

    def hidden_part(i, start, size):
        for copy in copies(i, start, size):
            copy.wait()
        cols = pl.ds(start, size)
        gate = dot_nn(x_out[...], w_gate[:, cols])
        upward = dot_nn(x_out[...], w_up[:, cols])
        grad = dot_nt(dy_out[...], w_down[cols, :])
        sigmoid = 1.0 / (1.0 + jnp.exp(-gate))
        passed = gate * sigmoid
        hid_out[:, cols] = (passed * upward).astype(BF16)
        dgate_out[:, cols] = (
            grad * upward * sigmoid * (1.0 + gate * (1.0 - sigmoid))
        ).astype(BF16)
        dup_out[:, cols] = (grad * passed).astype(BF16)

    full = hidden // tile

    @pl.loop(0, full)
    def _(i):
        hidden_part(i, pl.multiple_of(i * tile, tile), tile)

    if full < len(spans):
        hidden_part(full, *spans[full])

    def width_part(n, dg):
        cols = pl.ds(pl.multiple_of(n * tile, tile), tile)
        result = dot_nn(hid_out[...], w_down[:, cols])
        grad = dot_nt(dgate_out[...], w_gate[cols, :]) + dot_nt(dup_out[...], w_up[cols, :])
        dx_a[:, cols] = grad[:half].astype(BF16)
        dx_b[:, cols] = grad[half:].astype(BF16)
        scaled = (result * gates[...]).astype(BF16)
        out_a[:, cols] = scaled[:half]
        out_b[:, cols] = scaled[half:]
        raw = jnp.concatenate([raw_a[:, cols], raw_b[:, cols]], axis=0).astype(F32)
        return dg + jnp.sum(raw * result, axis=-1, keepdims=True)

    dg_out[...] = lax.fori_loop(0, width // tile, width_part, jnp.zeros((2 * half, 1), F32))


def expert_rows(mine, tokens, grads, router, w_gate, w_up, w_down):
    half, width = tokens[0].shape
    hidden = w_gate.shape[2]
    rows = 2 * half
    parts = -(-hidden // 256)
    vmem = pl.BlockSpec(memory_space=pltpu.VMEM)
    shapes = [(rows, width)] * 2 + [(rows, hidden)] * 3 + [(half, width)] * 4
    return pl.pallas_call(
        functools.partial(expert_kernel, TOP),
        in_specs=[pl.BlockSpec(memory_space=pltpu.SMEM)]
        + [vmem] * 5
        + [pl.BlockSpec(memory_space=pl.ANY)] * 3,
        out_specs=[vmem] * 10,
        out_shape=[jax.ShapeDtypeStruct(shape, BF16) for shape in shapes]
        + [jax.ShapeDtypeStruct((rows, 1), F32)],
        scratch_shapes=[
            pltpu.VMEM((width, hidden), BF16),
            pltpu.VMEM((width, hidden), BF16),
            pltpu.VMEM((hidden, width), BF16),
            pltpu.VMEM((rows, 1), F32),
            pltpu.SemaphoreType.DMA((3, parts)),
        ],
        compiler_params=pltpu.CompilerParams(vmem_limit_bytes=60 * 1024 * 1024),
        cost_estimate=pl.CostEstimate(
            flops=12 * rows * width * hidden,
            transcendentals=rows * hidden,
            bytes_accessed=2 * (3 * width * hidden + 8 * rows * width + 3 * rows * hidden),
        ),
    )(mine, *tokens, *grads, router, w_gate, w_up, w_down)


def half_kernel(half_ref, far_in, near_in, *refs):
    count = 1
    fars, nears = refs[:count], refs[count : 2 * count]
    outs = refs[-count:]
    for j in range(count):
        total = dot_tn(far_in[...], fars[j][...]) + dot_tn(near_in[...], nears[j][...])
        if len(refs) > 3 * count:
            total = total + refs[2 * count + j][...].astype(F32)
        outs[j][...] = total.astype(outs[j].dtype)


def half_grads(far_in, near_in, far_grad, near_grad, half, received=None):
    depth, width = far_in.shape
    columns = far_grad.shape[1]
    tile = 512
    steps = width // 2 // tile
    taken = pl.BlockSpec((depth, tile), lambda i, half: (0, half[0] * steps + i))
    whole = pl.BlockSpec((depth, columns), lambda i, half: (0, 0))
    out = pl.BlockSpec((tile, columns), lambda i, half: (i, 0))
    operands = [far_in, near_in, far_grad, near_grad]
    specs = [taken] * 2 + [whole] * 2
    kind = BF16
    if received is not None:
        operands.append(received)
        specs.append(out)
        kind = F32
    return pl.pallas_call(
        half_kernel,
        grid_spec=pltpu.PrefetchScalarGridSpec(
            num_scalar_prefetch=1, grid=(steps,), in_specs=specs, out_specs=[out]
        ),
        out_shape=[jax.ShapeDtypeStruct((width // 2, columns), kind)],
        cost_estimate=pl.CostEstimate(
            flops=2 * depth * width * columns,
            transcendentals=0,
            bytes_accessed=2 * (depth * width + 2 * depth * columns + width * columns),
        ),
    )(half, *operands)[0]


def down_kernel(rank_ref, far_in, near_in, far_grad, near_grad, theirs, mine, total):
    half = theirs.shape[0]
    total[...] = dot_tn(far_in[...], far_grad[...]) + dot_tn(near_in[...], near_grad[...])
    rank = rank_ref[0]
    theirs[...] = total[pl.ds(pl.multiple_of((1 - rank) * half, 8), half), :].astype(BF16)
    mine[...] = total[pl.ds(pl.multiple_of(rank * half, 8), half), :].astype(BF16)


def down_grads(far_in, near_in, far_grad, near_grad, rank, side):
    depth, rows = far_in.shape
    width = far_grad.shape[1] // 2
    tile = 1024
    whole = pl.BlockSpec((depth, rows), lambda i, rank: (0, 0))
    piece = pl.BlockSpec((depth, tile), lambda i, rank: (0, side * (width // tile) + i))
    out = pl.BlockSpec((rows // 2, tile), lambda i, rank: (0, i))
    return pl.pallas_call(
        down_kernel,
        grid_spec=pltpu.PrefetchScalarGridSpec(
            num_scalar_prefetch=1,
            grid=(width // tile,),
            in_specs=[whole] * 2 + [piece] * 2,
            out_specs=[out] * 2,
            scratch_shapes=[pltpu.VMEM((rows, tile), F32)],
        ),
        out_shape=[jax.ShapeDtypeStruct((rows // 2, width), BF16)] * 2,
        cost_estimate=pl.CostEstimate(
            flops=4 * depth * rows * width,
            transcendentals=0,
            bytes_accessed=4 * depth * (rows + width) + 2 * rows * width,
        ),
    )(rank, far_in, near_in, far_grad, near_grad)


def merge_kernel(mine_a, mine_b, got_a, got_b, out):
    half = mine_a.shape[1]
    for j, (mine, got) in enumerate(((mine_a, got_a), (mine_b, got_b))):
        total = mine[...].astype(F32) + got[...].astype(F32)
        out[:, j * half : (j + 1) * half] = total


def merge_down(*parts):
    rows, half = parts[0].shape
    tile = rows // 4
    return pl.pallas_call(
        merge_kernel,
        grid=(4,),
        in_specs=[pl.BlockSpec((tile, half), lambda i: (i, 0))] * 4,
        out_specs=pl.BlockSpec((tile, 2 * half), lambda i: (i, 0)),
        out_shape=jax.ShapeDtypeStruct((rows, 2 * half), F32),
        cost_estimate=pl.CostEstimate(
            flops=0, transcendentals=0, bytes_accessed=16 * rows * half
        ),
    )(*parts)


def after(value, *others):
    return lax.optimization_barrier((value, *others))[0]


def layer(
    hidden_in,
    out_grad,
    routes,
    block_order,
    norm_attn,
    w_query,
    w_kv_down,
    norm_latent,
    w_key_up,
    w_value_up,
    w_out,
    norm_ffn,
    w_router,
    shared_gate,
    shared_up,
    shared_down,
    expert_gate,
    expert_up,
    expert_down,
):
    seqs, piece, width = hidden_in.shape
    n_expert = lax.axis_size(EXPERT)
    n_ctx = lax.axis_size(CTX)
    n_dp = lax.axis_size(DP)
    lanes = n_expert // 2
    heads = w_query.shape[1] // (NOPE + ROPE)
    expert_count = w_router.shape[1]
    slots = 8 * ((piece * TOP + 6 * expert_count - 1) // (6 * expert_count))
    expert_rank = lax.axis_index(EXPERT)
    ctx_rank = lax.axis_index(CTX)
    dp_rank = lax.axis_index(DP)
    span = piece * n_expert
    total_rows = span * n_ctx
    scale = (NOPE + ROPE) ** (-0.5)
    group = lanes * piece
    group_slots = lanes * slots

    def shift(value, steps):
        pairs = [(e, (e + 2 * steps) % n_expert) for e in range(n_expert)]
        return lax.ppermute(value, EXPERT, pairs)

    def across(value):
        return lax.ppermute(value, EXPERT, [(e, e ^ 1) for e in range(n_expert)])

    def other_dp(value):
        return lax.ppermute(value, DP, [(d, n_dp - 1 - d) for d in range(n_dp)])

    def other_ctx(value):
        return lax.ppermute(value, CTX, [(c, n_ctx - 1 - c) for c in range(n_ctx)])

    up_count = lanes // 2
    down_count = lanes - 1 - up_count

    def gather_blocks(own):
        ups, downs = [own], [own]
        for k in range(max(up_count, down_count)):
            if k < up_count:
                ups.append(shift(ups[-1], 1))
            if k < down_count:
                downs.append(shift(downs[-1], -1))
        column = ups + downs[:0:-1]
        return column + [across(b) for b in column]

    def gather_ctx(value):
        if n_ctx == 2:
            return [value, other_ctx(value)], [ctx_rank, 1 - ctx_rank]
        return [lax.all_gather(value, CTX, axis=1, tiled=True)], list(range(n_ctx))

    def scatter_ctx(value):
        if n_ctx == 2:
            half = value.shape[1] // 2
            return add(value[:, :half], other_ctx(value[:, half:]))
        return lax.psum_scatter(value, CTX, scatter_dimension=1, tiled=True)

    def add(*terms):
        total = terms[0].astype(F32)
        for term in terms[1:]:
            total = total + term.astype(F32)
        return total.astype(BF16)

    def scatter_blocks(part, hold=()):
        order = [up_count] + [k for k in range(lanes - 1, 0, -1) if k != up_count] + [0]
        crossed = {k: across(part(lanes + k)) for k in order}
        sums = {k: (part(k), crossed[k]) for k in order}
        marks = [crossed[up_count]]
        moving = add(*sums[up_count])
        for k in range(up_count, 0, -1):
            if k == 1 and hold:
                moving = after(moving, *hold)
            moving = shift(moving, -1)
            marks.append(moving)
            if k > 1:
                moving = add(*sums[k - 1], moving)
        result = [*sums[0], moving]
        if down_count:
            moving = add(*sums[lanes - down_count])
            for d in range(down_count, 0, -1):
                moving = shift(moving, 1)
                if d > 1:
                    moving = add(*sums[lanes - d + 1], moving)
            result.append(moving)
        return sum(term.astype(F32) for term in result), marks

    def sum_copies(grad, small=False):
        sent = grad.astype(BF16)
        if n_ctx != 2:
            return lax.psum(sent, (DP, CTX)).astype(F32)
        if small:
            pair = add(sent, other_ctx(sent))
            return pair.astype(F32) + other_dp(pair).astype(F32)
        half = grad.shape[0] // 2
        mine = lax.dynamic_slice_in_dim(sent, ctx_rank * half, half, 0)
        theirs = lax.dynamic_slice_in_dim(sent, (1 - ctx_rank) * half, half, 0)
        pair = add(mine, other_ctx(theirs))
        full = add(pair, other_dp(pair))
        rest = other_ctx(full)
        first = ctx_rank == 0
        return jnp.concatenate(
            [jnp.where(first, full, rest), jnp.where(first, rest, full)], axis=0
        ).astype(F32)

    def split_copies(grad):
        return lax.psum_scatter(
            grad.astype(BF16), CTX, scatter_dimension=0, tiled=True
        ).astype(F32)

    rank_z, rank_x = expert_rank // 2, expert_rank % 2
    owners = [
        ((rank_z - j % lanes) % lanes) * 2 + (rank_x + j // lanes) % 2 for j in range(n_expert)
    ]
    owner_ids = jnp.stack(owners)
    ids = jnp.arange(n_expert, dtype=jnp.int32)
    block_of = ((ids % 2 + rank_x) % 2) * lanes + (rank_z - ids // 2) % lanes

    tail = 2 * ROPE
    routes_tail = jnp.pad(routes.astype(BF16), ((0, 0), (0, 0), (0, tail - TOP)))
    blocks = gather_blocks(jnp.concatenate([hidden_in, routes_tail], axis=-1))

    kv_rows = w_kv_down.shape[0]
    kv_piece = kv_rows // n_ctx
    kv_own = lax.dynamic_slice_in_dim(w_kv_down, ctx_rank * kv_piece, kv_piece, 0)
    kv_blocks = gather_blocks(kv_own)
    kv_span = join([b[None] for b in kv_blocks])
    kv_all, ctx_ranks = gather_ctx(kv_span)
    ctx_ranks = jnp.stack([jnp.asarray(r, jnp.int32) for r in ctx_ranks])
    kv_dest = (owner_ids[None, :] * n_ctx + ctx_ranks[:, None]).reshape(-1)
    kv_full = place(kv_all, kv_dest, kv_piece)[0]

    def rms(rows):
        return lax.rsqrt(jnp.mean(rows * rows, axis=-1, keepdims=True) + EPSILON)

    half_rows = total_rows // (2 * n_ctx)

    def positions(row_ids):
        matches = (row_ids // half_rows)[:, None] == jnp.arange(2 * n_ctx, dtype=jnp.int32)
        starts = jnp.sum(jnp.where(matches[None], block_order[:, None, :], 0), axis=2)
        return starts * half_rows + row_ids % half_rows

    piece_ids = jnp.arange(piece, dtype=jnp.int32)
    in_span = (owner_ids[:, None] * piece + piece_ids[None, :]).reshape(-1)
    span_pos = positions(ctx_rank * span + in_span)
    key_pos = positions((ctx_ranks[:, None] * span + in_span[None, :]).reshape(-1))
    tables = rope_tables(span_pos)
    span_cos, span_sin = tables
    turns = jnp.concatenate([span_cos, span_cos, span_sin, span_sin], axis=-1)
    span_cos = jnp.tile(span_cos, (1, 1, 2 * heads))
    span_sin = jnp.tile(span_sin, (1, 1, 2 * heads))

    per_head = w_query.reshape(width, heads, NOPE + ROPE)
    w_nope = per_head[..., :NOPE].reshape(width, heads * NOPE)
    w_rope = per_head[..., NOPE:]
    first, second = halves(w_rope)
    w_turned = jnp.concatenate([-second, first], axis=-1).reshape(width, heads * ROPE)
    w_inner = jnp.concatenate([w_nope, w_rope.reshape(width, heads * ROPE), w_turned], axis=-1)
    w_up = jnp.concatenate([w_key_up, w_value_up], axis=-1)
    shared_width = shared_gate.shape[1]
    shared_room = -(-shared_width // 128) * 128
    spare = ((0, shared_room - shared_width), (0, 0))
    w_shared = jnp.concatenate([jnp.pad(shared_gate.T, spare), jnp.pad(shared_up.T, spare)], axis=0)
    w_shared_down = jnp.pad(shared_down, spare)
    w_inner, w_up, w_shared, w_shared_down = lax.optimization_barrier(
        (w_inner, w_up, w_shared, w_shared_down)
    )

    own_rows = hidden_in.astype(F32)
    inv_own = rms(own_rows)
    normed_span, routes_cols = join_norm(blocks, norm_attn)
    grad_all = lax.all_gather(after(out_grad, normed_span), EXPERT, axis=1, tiled=True)
    kv_joint = product(normed_span, kv_full)
    latent_raw = kv_joint[..., :LATENT]
    inv_latent = rms(latent_raw)
    key_rope = rotate(kv_joint[..., LATENT:], tables)
    rope_first, rope_second = halves(key_rope)
    latent_span = jnp.concatenate(
        [latent_raw * inv_latent * norm_latent, key_rope, rope_second, -rope_first], axis=-1
    ).astype(BF16)
    latent_all = gather_ctx(latent_span)[0]
    latent_all = jnp.concatenate(latent_all, axis=1) if len(latent_all) > 1 else latent_all[0]
    query_raw = product(normed_span, w_inner)
    flat = heads * NOPE
    queries = jnp.concatenate(
        [
            query_raw[..., :flat],
            query_raw[..., flat : flat + heads * ROPE] * span_cos
            + query_raw[..., flat + heads * ROPE :] * span_sin,
        ],
        axis=-1,
    ).astype(BF16)
    latent_part = latent_all[..., :LATENT]
    pairs = product(latent_part, w_up).astype(BF16)
    heads_out, lse = attend(queries, pairs, latent_all, span_pos, key_pos, heads, scale)

    def block_of_span(array, j):
        return array[:, j * piece : (j + 1) * piece]

    routes_span = routes_cols[..., :TOP].astype(jnp.int32).reshape(seqs, n_expert, piece, TOP)
    mine = dp_rank * n_expert + expert_rank
    theirs = (n_dp - 1 - dp_rank) * n_expert + expert_rank
    earlier = (piece_ids[:, None] < piece_ids[None, :]).astype(F32)
    slot_ids = jnp.arange(slots, dtype=jnp.int32)
    picks = []
    for target in (mine, theirs):
        named = jnp.any(routes_span == target, axis=-1)
        rank = jnp.einsum("sjp,pq->sjq", named.astype(F32), earlier).astype(jnp.int32)
        picks.append(jnp.where(named, rank, -1)[:, :, None, :] == slot_ids[:, None])

    def side_tables(table):
        return [
            table[:, side * lanes : (side + 1) * lanes].reshape(seqs, group_slots, piece)
            for side in range(2)
        ]

    near_tables = side_tables(picks[0].astype(BF16))
    far_tables = side_tables(picks[1].astype(BF16))
    grad_span = place([grad_all], block_of, piece)
    grad_slots = [
        pick_span(grad_span, routes_cols, side, near_tables[side], far_tables[side])
        for side in range(2)
    ]
    grad_got = [other_dp(grad_slots[side][1]) for side in range(2)]
    sh_dhidden = back_product(grad_span, w_shared_down)

    def project_sides(rows, weight, transposed):
        far_side = project(rows, 1, weight, lanes, transposed)
        near_side = project(rows, 0, weight, lanes, transposed)
        return lambda j: (near_side, far_side)[j // lanes][j % lanes]

    attn_own, _ = scatter_blocks(
        project_sides(heads_out, w_out, False),
        hold=(sh_dhidden, grad_slots[0][1], grad_slots[1][1]),
    )
    residual = own_rows + attn_own
    inv_ffn = rms(residual)
    unit_ffn = residual * inv_ffn
    normed_ffn = (unit_ffn * norm_ffn).astype(BF16)
    ffn_blocks = gather_blocks(normed_ffn)
    token_slots = [
        pick_blocks(
            ffn_blocks[side * lanes : (side + 1) * lanes], near_tables[side], far_tables[side]
        )
        for side in range(2)
    ]
    token_got = [other_dp(token_slots[side][1]) for side in range(2)]
    ffn_span = join([after(b, token_slots[1][1]) for b in ffn_blocks])

    sh_both = back_product(ffn_span, w_shared)
    sh_gate, sh_up = sh_both[..., :shared_room], sh_both[..., shared_room:]
    sh_hidden = (jax.nn.silu(sh_gate) * sh_up).astype(BF16)
    sh_dboth = jnp.concatenate(silu_grads(sh_dhidden, sh_gate, sh_up), axis=-1)
    sh_dnorm = product(sh_dboth, w_shared).astype(BF16)

    slot_shape = (seqs, group_slots)

    def expert(tokens, grads):
        rows = [t.reshape(seqs * group_slots, -1) for t in (*tokens, *grads)]
        results = expert_rows(
            mine.reshape(1),
            rows[:2],
            rows[2:],
            w_router.T,
            expert_gate,
            expert_up,
            expert_down,
        )
        dx, out = [
            [side.reshape(*slot_shape, width) for side in pair]
            for pair in (results[5:7], results[7:9])
        ]
        return results[:5], dx, out, results[9].reshape(2, *slot_shape)

    far, far_dx, far_out, far_dg = expert([after(t, sh_dnorm) for t in token_got], grad_got)
    dg_back = other_dp(far_dg)
    dx_back = [None, None]
    dx_back[1] = other_dp(far_dx[1])
    dx_back[0] = other_dp(far_dx[0])
    out_back = [other_dp(after(far_out[side], *dx_back)) for side in range(2)]
    near, near_dx, near_out, near_dg = expert(
        [after(t[0], far_dx[1]) for t in token_slots], [g[0] for g in grad_slots]
    )

    lane_ids = jnp.arange(128, dtype=jnp.int32)

    def dg_columns(side):
        columns = 0.0
        for pick, dg, target in ((picks[0], near_dg, mine), (picks[1], dg_back, theirs)):
            table = pick[:, side * lanes : (side + 1) * lanes]
            values = dg[side].reshape(seqs, lanes, slots, 1)
            rows = jnp.sum(jnp.where(table, values, 0.0), axis=2).reshape(seqs, group, 1)
            top = rows.astype(BF16).astype(F32)
            columns = columns + jnp.where(lane_ids == target, top, 0.0)
            columns = columns + jnp.where(lane_ids == target + expert_count, rows - top, 0.0)
        return columns.astype(BF16)

    dnorm_blocks = [
        spread_blocks(
            sh_dnorm,
            side,
            near_tables[side],
            near_dx[side],
            far_tables[side],
            dx_back[side],
            dg_columns(side),
        )
        for side in range(2)
    ]
    dnorm_sum, marks = scatter_blocks(lambda j: dnorm_blocks[j // lanes][j % lanes])

    grad_sh_in = weight_grad(sh_dboth, ffn_span).astype(BF16)
    grad_sh_down = weight_grad(sh_hidden, grad_span).astype(BF16)
    grad_sh_in, grad_sh_down = lax.psum(
        (after(grad_sh_in, dnorm_blocks[0][0]), after(grad_sh_down, dnorm_blocks[0][0])),
        (DP, CTX),
    )

    dg_own = (
        dnorm_sum[..., width : width + expert_count]
        + dnorm_sum[..., width + expert_count : width + 2 * expert_count]
    )
    dnorm_sum = dnorm_sum[..., :width]
    route_hot = routes[..., None] == jnp.arange(expert_count, dtype=jnp.int32)
    logits = product(normed_ffn, w_router)
    chosen = jnp.sum(jnp.where(route_hot, logits[:, :, None, :], 0.0), axis=-1)
    gate_weights = jax.nn.softmax(chosen, axis=-1)
    grad_choice = jnp.sum(jnp.where(route_hot, dg_own[:, :, None, :], 0.0), axis=-1)
    grad_chosen = gate_weights * (
        grad_choice - jnp.sum(gate_weights * grad_choice, axis=-1, keepdims=True)
    )
    grad_logits = jnp.sum(jnp.where(route_hot, grad_chosen[..., None], 0.0), axis=2).astype(BF16)
    dnorm_ffn = dnorm_sum + back_product(grad_logits, w_router)
    grad_resid = out_grad.astype(F32) + norm_back(dnorm_ffn, residual, inv_ffn, norm_ffn)
    attn_blocks = gather_blocks(grad_resid.astype(BF16))
    grad_attn = join(attn_blocks)
    grad_router = weight_grad(normed_ffn, after(grad_logits, attn_blocks[1]))
    grad_gain_ffn = jnp.sum(after(dnorm_ffn, attn_blocks[1]) * unit_ffn, axis=(0, 1))

    sh_out = product(after(sh_hidden, marks[1]), w_shared_down).astype(BF16)
    out_blocks = []
    for side in range(2):
        out_blocks += spread_blocks(
            sh_out,
            side,
            near_tables[side],
            near_out[side],
            far_tables[side],
            out_back[side],
        )
    out_part = place(out_blocks, owner_ids, piece)
    out_own = lax.psum_scatter(out_part, EXPERT, scatter_dimension=1, tiled=True)
    out_hidden = (residual + out_own.astype(F32)).astype(BF16)

    if n_ctx == 2:
        rank = ctx_rank.reshape(1)
        ready = after(rank, dnorm_blocks[0][0])
        got = []
        for i in (3, 4):
            part = half_grads(far[0], near[0], far[i], near[i], 1 - ready)
            got.append(other_ctx(part))
        down_mine = []
        for side in range(2):
            part, own = down_grads(far[2], near[2], far[1], near[1], ready, side)
            got.append(other_ctx(part))
            down_mine.append(own)
    else:
        rows_in, grads_in, ex_hidden, ex_dgate, ex_dup = [
            jnp.concatenate([f, n], axis=0) for f, n in zip(far[:5], near[:5])
        ]
        exp_grads = [
            split_copies(weight_grad(rows_in, ex_dgate)),
            split_copies(weight_grad(rows_in, ex_dup)),
            split_copies(weight_grad(ex_hidden, grads_in)),
        ]

    grad_heads = back_product(grad_attn, w_out).astype(BF16)
    grad_queries, grad_pairs, grad_key_rope = attend_back(
        queries, pairs, latent_all, grad_heads, lse, span_pos, key_pos, turns, heads, scale
    )
    grad_latent = jnp.concatenate(
        [back_product(grad_pairs, w_up).astype(BF16), grad_key_rope], axis=-1
    )

    def by_rank(array):
        return array.reshape(n_expert, -1)

    def padded(array, size):
        return jnp.pad(array, ((0, 0), (0, size - array.shape[1])))

    room = seqs * piece * ROPE
    early = jnp.concatenate([by_rank(grad_gain_ffn), by_rank(grad_router)], axis=1)
    early_size = early.shape[1]
    early = jnp.take(padded(early, room).astype(BF16), owner_ids, axis=0, mode="clip")
    early = early.reshape(n_expert, seqs, piece, ROPE).transpose(1, 0, 2, 3)
    grad_latent_span = jnp.concatenate(
        [scatter_ctx(grad_latent), early.reshape(seqs, span, ROPE)], axis=-1
    )
    dnorm_own, marks = scatter_blocks(project_sides(grad_queries, w_query, True))
    grad_latent_own, lat_marks = scatter_blocks(lambda j: block_of_span(grad_latent_span, j))
    early = grad_latent_own[..., LATENT + ROPE :].reshape(-1)[:early_size]

    grad_query_part = weight_grad(normed_span, after(grad_queries, lat_marks[1]))
    grad_up_part = weight_grad(latent_part, after(grad_pairs, lat_marks[1]))
    grad_out_part = weight_grad(heads_out, grad_attn)
    grad_query_w = sum_copies(grad_query_part)
    grad_out_w = sum_copies(grad_out_part)
    grad_up = sum_copies(grad_up_part, small=True)
    if n_ctx == 2:
        exp_grads = []
        for i in range(2):
            exp_grads.append(
                half_grads(far[0], near[0], far[3 + i], near[3 + i], after(rank, marks[0]), got[i])
            )
    gain_part = jnp.sum(grad_query_part * w_query.astype(F32), axis=-1) / norm_attn
    gain_latent_part = jnp.sum(grad_up_part * w_up.astype(F32), axis=-1) / norm_latent
    late = jnp.concatenate([by_rank(gain_part), by_rank(gain_latent_part)], axis=1)
    late_size = late.shape[1]
    late = padded(late.reshape(1, -1), room).astype(BF16).reshape(seqs, piece, ROPE)

    grad_unit = grad_latent_own[..., :LATENT]
    own_tables = [table[:, :piece] for table in tables]
    grad_kv = jnp.concatenate(
        [
            norm_back(grad_unit, latent_raw[:, :piece], inv_latent[:, :piece], norm_latent),
            unrotate(grad_latent_own[..., LATENT : LATENT + ROPE], own_tables),
        ],
        axis=-1,
    ).astype(BF16)
    kv_grads = gather_blocks(jnp.concatenate([grad_kv, late], axis=-1))
    grad_kv_span = join(kv_grads)
    shared_sums = lax.optimization_barrier(
        (grad_sh_in, grad_sh_down, kv_grads[lanes + up_count])
    )[:2]
    if n_ctx == 2:
        exp_grads.append(merge_down(*down_mine, *got[2:]))
    dnorm_kv = back_product(grad_kv, kv_full)
    in_grad = (
        grad_resid + norm_back(dnorm_own + dnorm_kv, own_rows, inv_own, norm_attn)
    ).astype(BF16)
    normed_cols = lax.dynamic_slice_in_dim(normed_span, expert_rank * kv_rows, kv_rows, 2)
    late = (
        grad_kv_span[..., LATENT + ROPE :]
        .reshape(seqs, n_expert, piece, ROPE)
        .transpose(1, 0, 2, 3)
        .reshape(n_expert, -1)[:, : n_expert * late_size]
        .reshape(n_expert, n_expert, late_size)
    )
    late = jnp.sum(
        lax.dynamic_index_in_dim(late, expert_rank, 1, False).astype(F32), axis=0
    )
    rows = width // n_expert
    small = padded(jnp.concatenate([late, early])[None], kv_rows * ROPE).reshape(kv_rows, ROPE)
    kv_small = sum_copies(
        jnp.concatenate(
            [weight_grad(normed_cols, grad_kv_span[..., : LATENT + ROPE]), small], axis=-1
        ),
        small=True,
    )
    grad_kv_w = kv_small[:, : LATENT + ROPE]
    small = kv_small[:, LATENT + ROPE :].reshape(-1)
    late, early = small[:late_size], small[late_size : late_size + early_size]
    own_gain = lax.dynamic_slice_in_dim(norm_attn, expert_rank * rows, rows, 0)
    gain_kv = jnp.sum(grad_kv_w * w_kv_down.astype(F32), axis=-1) / own_gain
    return (
        out_hidden,
        in_grad,
        late[:rows] + gain_kv,
        grad_query_w,
        grad_kv_w,
        late[rows:],
        grad_up[:, :flat],
        grad_up[:, flat:],
        grad_out_w,
        early[:rows],
        early[rows:].reshape(rows, expert_count),
        shared_sums[0][:shared_width].astype(F32).T,
        shared_sums[0][shared_room : shared_room + shared_width].astype(F32).T,
        shared_sums[1][:shared_width].astype(F32),
        exp_grads[0][None],
        exp_grads[1][None],
        exp_grads[2][None],
    )


def solution(mesh):
    return jax.shard_map(
        layer,
        mesh=mesh,
        in_specs=(
            P(DP, (CTX, EXPERT), None),
            P(DP, (CTX, EXPERT), None),
            P(DP, (CTX, EXPERT), None),
            P(DP, None),
            P(),
            P(None, EXPERT),
            P(EXPERT, None),
            P(),
            P(None, EXPERT),
            P(None, EXPERT),
            P(EXPERT, None),
            P(),
            P(),
            P(None, EXPERT),
            P(None, EXPERT),
            P(EXPERT, None),
            P((DP, EXPERT), None, None),
            P((DP, EXPERT), None, None),
            P((DP, EXPERT), None, None),
        ),
        out_specs=(
            P(DP, (CTX, EXPERT), None),
            P(DP, (CTX, EXPERT), None),
            P(EXPERT),
            P(None, EXPERT),
            P(EXPERT, None),
            P(EXPERT),
            P(None, EXPERT),
            P(None, EXPERT),
            P(EXPERT, None),
            P(EXPERT),
            P(EXPERT, None),
            P(None, EXPERT),
            P(None, EXPERT),
            P(EXPERT, None),
            P((DP, EXPERT), CTX, None),
            P((DP, EXPERT), CTX, None),
            P((DP, EXPERT), CTX, None),
        ),
        check_vma=False,
    )
```

```python
import functools

import jax
import jax.numpy as jnp
from jax import lax
from jax.experimental import pallas as pl
from jax.experimental.pallas import tpu as pltpu
from jax.sharding import PartitionSpec as P


NOPE = 128
ROPE = 64
VDIM = 128
LATENT = 512
TOP = 6
EPSILON = 1e-06
MASKED = -1e30
BF16 = jnp.bfloat16
F32 = jnp.float32
EXPERT, CTX, DP = "expert", "ctx", "dp"


def product(inputs, matrix):
    return jnp.dot(inputs, matrix, preferred_element_type=F32)


def back_product(gradient, matrix):
    return lax.dot_general(
        gradient,
        matrix,
        (((gradient.ndim - 1,), (1,)), ((), ())),
        preferred_element_type=F32,
    )


def weight_grad(inputs, gradient):
    flat_in = inputs.reshape(-1, inputs.shape[-1])
    flat_grad = gradient.reshape(-1, gradient.shape[-1])
    return lax.dot_general(
        flat_in, flat_grad, (((0,), (0,)), ((), ())), preferred_element_type=F32
    )


def rope_tables(positions):
    inverse = 10000.0 ** (-2.0 * jnp.arange(ROPE // 2, dtype=F32) / ROPE)
    angles = positions.astype(F32)[..., None] * inverse
    return jnp.cos(angles), jnp.sin(angles)


def halves(vectors):
    return vectors[..., : ROPE // 2], vectors[..., ROPE // 2 :]


def rotate(vectors, tables):
    first, second = halves(vectors)
    cosine, sine = tables
    return jnp.concatenate(
        [first * cosine - second * sine, second * cosine + first * sine], axis=-1
    )


def unrotate(gradient, tables):
    first, second = halves(gradient)
    cosine, sine = tables
    return jnp.concatenate(
        [first * cosine + second * sine, second * cosine - first * sine], axis=-1
    )


def norm_back(gradient, inputs, inverse_rms, gain_vec):
    scaled = gradient * gain_vec
    return inverse_rms * scaled - inputs * inverse_rms**3 * jnp.mean(
        inputs * scaled, axis=-1, keepdims=True
    )


def silu_grads(grad_hidden, gate, upward):
    sigmoid_gate = jax.nn.sigmoid(gate)
    grad_gate = grad_hidden * upward * sigmoid_gate * (1.0 + gate * (1.0 - sigmoid_gate))
    grad_upward = grad_hidden * gate * sigmoid_gate
    return (grad_gate.astype(BF16), grad_upward.astype(BF16))


def dot_nt(left, right):
    return lax.dot_general(left, right, (((1,), (1,)), ((), ())), preferred_element_type=F32)


def dot_tn(left, right):
    return lax.dot_general(left, right, (((0,), (0,)), ((), ())), preferred_element_type=F32)


def dot_nn(left, right):
    return lax.dot_general(left, right, (((1,), (0,)), ((), ())), preferred_element_type=F32)


def head_cols(head):
    return slice(head * NOPE, (head + 1) * NOPE)


def rope_cols(heads, head):
    start = heads * NOPE + head * ROPE
    return slice(start, start + ROPE)


def forward_kernel(heads, scale, q_ref, k_ref, v_ref, kr_ref, pq_ref, pk_ref, o_ref, lse_ref):
    allowed = pk_ref[0] <= pq_ref[0]
    for head in range(heads):
        cols = head_cols(head)
        scores = dot_nt(k_ref[0, :, cols], q_ref[0, :, cols])
        scores = scores + dot_nt(kr_ref[0, :, :ROPE], q_ref[0, :, rope_cols(heads, head)])
        scores = jnp.where(allowed, scores * scale, MASKED)
        top = jnp.max(scores, axis=0, keepdims=True)
        weights = jnp.exp(scores - top)
        total = jnp.sum(weights, axis=0, keepdims=True)
        lse_ref[0, head : head + 1, :] = top + jnp.log(total)
        probs = (weights * (1.0 / total)).astype(BF16)
        o_ref[0, :, cols] = dot_tn(probs, v_ref[0, :, cols]).astype(BF16)


def backward_kernel(
    heads,
    scale,
    q_ref,
    k_ref,
    v_ref,
    kr_ref,
    do_ref,
    lse_ref,
    pq_ref,
    pk_ref,
    turn_ref,
    dq_ref,
    dkv_ref,
    dkr_ref,
    dkv_acc,
    dkr_acc,
):
    step = pl.program_id(1)

    @pl.when(step == 0)
    def _():
        dkv_acc[...] = jnp.zeros_like(dkv_acc)
        dkr_acc[...] = jnp.zeros_like(dkr_acc)

    allowed = pk_ref[0] <= pq_ref[0]
    pieces = []
    for head in range(heads):
        cols = head_cols(head)
        value_cols = head_cols(heads + head)
        keys = k_ref[0, :, cols]
        query = q_ref[0, :, cols]
        query_rope = q_ref[0, :, rope_cols(heads, head)]
        grad = do_ref[0, :, cols]
        scores = dot_nt(keys, query) + dot_nt(kr_ref[0, :, :ROPE], query_rope)
        probs = jnp.where(
            allowed, jnp.exp(scores * scale - lse_ref[0, head : head + 1, :]), 0.0
        )
        grad_probs = dot_nt(v_ref[0, :, cols], grad)
        inner = jnp.sum(probs * grad_probs, axis=0, keepdims=True)
        grad_raw = (probs * (grad_probs - inner) * scale).astype(BF16)
        dkv_acc[:, value_cols] += dot_nn(probs.astype(BF16), grad)
        dkv_acc[:, cols] += dot_nn(grad_raw, query)
        dkr_acc[...] += dot_nn(grad_raw, query_rope)
        turned = dot_tn(grad_raw, kr_ref[0]) * turn_ref[0]
        pieces.append(dot_tn(grad_raw, keys))
        pieces.append(turned[:, :ROPE] + turned[:, ROPE:])
    dq_ref[0] = jnp.concatenate(pieces, axis=1).astype(BF16)

    @pl.when(step == pl.num_programs(1) - 1)
    def _():
        dkv_ref[0] = dkv_acc[...].astype(BF16)
        dkr_ref[0] = dkr_acc[...].astype(BF16)


def query_tile(rows, total_rows):
    return min(rows, max(128, 256 * 1024 // total_rows))


def attend(queries, pairs, key_rope, pos_q, pos_k, heads, scale):
    seqs, rows, width = queries.shape
    total_rows = pairs.shape[1]
    tile = query_tile(rows, total_rows)
    flat = heads * NOPE
    return pl.pallas_call(
        functools.partial(forward_kernel, heads, scale),
        grid=(seqs, rows // tile),
        in_specs=[
            pl.BlockSpec((1, tile, width), lambda s, i: (s, i, 0)),
            pl.BlockSpec((1, total_rows, flat), lambda s, i: (s, 0, 0)),
            pl.BlockSpec((1, total_rows, flat), lambda s, i: (s, 0, 1)),
            pl.BlockSpec((1, total_rows, 2 * ROPE), lambda s, i: (s, 0, LATENT // (2 * ROPE))),
            pl.BlockSpec((1, 1, tile), lambda s, i: (s, 0, i)),
            pl.BlockSpec((1, total_rows, 1), lambda s, i: (s, 0, 0)),
        ],
        out_specs=[
            pl.BlockSpec((1, tile, flat), lambda s, i: (s, i, 0)),
            pl.BlockSpec((1, heads, tile), lambda s, i: (s, 0, i)),
        ],
        out_shape=[
            jax.ShapeDtypeStruct((seqs, rows, flat), BF16),
            jax.ShapeDtypeStruct((seqs, heads, rows), F32),
        ],
        cost_estimate=pl.CostEstimate(
            flops=2 * seqs * heads * rows * total_rows * (NOPE + ROPE + VDIM),
            transcendentals=seqs * heads * rows * total_rows,
            bytes_accessed=2 * seqs * (rows * width + 2 * total_rows * flat),
        ),
    )(queries, pairs, pairs, key_rope, pos_q[:, None, :], pos_k[:, :, None])


def attend_back(queries, pairs, key_rope, grads, lse, pos_q, pos_k, turns, heads, scale):
    seqs, rows, width = queries.shape
    total_rows = pairs.shape[1]
    tile = query_tile(rows, total_rows)
    flat = heads * NOPE
    whole = lambda s, i: (s, 0, 0)
    piece = lambda s, i: (s, i, 0)
    return pl.pallas_call(
        functools.partial(backward_kernel, heads, scale),
        grid=(seqs, rows // tile),
        in_specs=[
            pl.BlockSpec((1, tile, width), piece),
            pl.BlockSpec((1, total_rows, flat), whole),
            pl.BlockSpec((1, total_rows, flat), lambda s, i: (s, 0, 1)),
            pl.BlockSpec((1, total_rows, 2 * ROPE), lambda s, i: (s, 0, LATENT // (2 * ROPE))),
            pl.BlockSpec((1, tile, flat), piece),
            pl.BlockSpec((1, heads, tile), lambda s, i: (s, 0, i)),
            pl.BlockSpec((1, 1, tile), lambda s, i: (s, 0, i)),
            pl.BlockSpec((1, total_rows, 1), whole),
            pl.BlockSpec((1, tile, 2 * ROPE), piece),
        ],
        out_specs=[
            pl.BlockSpec((1, tile, width), piece),
            pl.BlockSpec((1, total_rows, 2 * flat), whole),
            pl.BlockSpec((1, total_rows, ROPE), whole),
        ],
        out_shape=[
            jax.ShapeDtypeStruct((seqs, rows, width), BF16),
            jax.ShapeDtypeStruct((seqs, total_rows, 2 * flat), BF16),
            jax.ShapeDtypeStruct((seqs, total_rows, ROPE), BF16),
        ],
        scratch_shapes=[
            pltpu.VMEM((total_rows, 2 * flat), F32),
            pltpu.VMEM((total_rows, ROPE), F32),
        ],
        cost_estimate=pl.CostEstimate(
            flops=4 * seqs * heads * rows * total_rows * (NOPE + ROPE + VDIM),
            transcendentals=seqs * heads * rows * total_rows,
            bytes_accessed=2 * seqs * (rows * width + 4 * total_rows * flat),
        ),
    )(
        queries, pairs, pairs, key_rope, grads, lse, pos_q[:, None, :], pos_k[:, :, None], turns
    )


def join_kernel(count, *refs):
    rows = refs[0].shape[1]
    for j in range(count):
        refs[count][0, j * rows : (j + 1) * rows, :] = refs[j][0]


def join_norm_kernel(count, width, *refs):
    gain, out, tail = refs[count][...], refs[count + 1], refs[count + 2]
    rows = refs[0].shape[1]
    for j in range(count):
        values = refs[j][0, :, :width].astype(F32)
        inverse = lax.rsqrt(jnp.mean(values * values, axis=-1, keepdims=True) + EPSILON)
        part = slice(j * rows, (j + 1) * rows)
        out[0, part, :] = (values * inverse * gain).astype(BF16)
        tail[0, part, :] = refs[j][0, :, width:]


def join_norm(blocks, gain):
    seqs, rows, total = blocks[0].shape
    width = gain.shape[0]
    count = len(blocks)
    first = lambda s: (s, 0, 0)
    return pl.pallas_call(
        functools.partial(join_norm_kernel, count, width),
        grid=(seqs,),
        in_specs=[pl.BlockSpec((1, rows, total), first)] * count
        + [pl.BlockSpec((1, width), lambda s: (0, 0))],
        out_specs=[
            pl.BlockSpec((1, count * rows, width), first),
            pl.BlockSpec((1, count * rows, total - width), first),
        ],
        out_shape=[
            jax.ShapeDtypeStruct((seqs, count * rows, width), BF16),
            jax.ShapeDtypeStruct((seqs, count * rows, total - width), BF16),
        ],
        cost_estimate=pl.CostEstimate(
            flops=0, transcendentals=0, bytes_accessed=4 * seqs * count * rows * total
        ),
    )(*blocks, gain[None])


def join(blocks):
    seqs, rows, width = blocks[0].shape
    count = len(blocks)
    return pl.pallas_call(
        functools.partial(join_kernel, count),
        grid=(seqs,),
        in_specs=[pl.BlockSpec((1, rows, width), lambda s: (s, 0, 0))] * count,
        out_specs=pl.BlockSpec((1, count * rows, width), lambda s: (s, 0, 0)),
        out_shape=jax.ShapeDtypeStruct((seqs, count * rows, width), BF16),
        cost_estimate=pl.CostEstimate(
            flops=0, transcendentals=0, bytes_accessed=4 * seqs * count * rows * width
        ),
    )(*blocks)


def pick_kernel(count, slots, *refs):
    near, far = refs[count + 2], refs[count + 3]
    for j in range(count):
        rows = refs[j][0]
        part = slice(j * slots, (j + 1) * slots)
        near[0, part, :] = dot_nn(refs[count][0, part, :], rows).astype(BF16)
        far[0, part, :] = dot_nn(refs[count + 1][0, part, :], rows).astype(BF16)


def pick_blocks(blocks, near, far):
    seqs, rows, width = blocks[0].shape
    count = len(blocks)
    total = near.shape[1]
    block = pl.BlockSpec((1, rows, width), lambda s: (s, 0, 0))
    table = pl.BlockSpec((1, total, rows), lambda s: (s, 0, 0))
    out = pl.BlockSpec((1, total, width), lambda s: (s, 0, 0))
    return pl.pallas_call(
        functools.partial(pick_kernel, count, total // count),
        grid=(seqs,),
        in_specs=[block] * count + [table] * 2,
        out_specs=[out] * 2,
        out_shape=[jax.ShapeDtypeStruct((seqs, total, width), BF16)] * 2,
        cost_estimate=pl.CostEstimate(
            flops=4 * seqs * total * rows * width,
            transcendentals=0,
            bytes_accessed=2 * seqs * (count * rows + 2 * total) * width,
        ),
    )(*blocks, near, far)


def pick_span_kernel(count, slots, rows_ref, tail_ref, near_ref, far_ref, near, far):
    piece = rows_ref.shape[1] // count
    width = rows_ref.shape[2]
    for j in range(count):
        own = slice(j * piece, (j + 1) * piece)
        part = slice(j * slots, (j + 1) * slots)
        for table, out in ((near_ref, near), (far_ref, far)):
            picks = table[0, part, :]
            out[0, part, :width] = dot_nn(picks, rows_ref[0, own, :]).astype(BF16)
            out[0, part, width:] = dot_nn(picks, tail_ref[0, own, :]).astype(BF16)


def pick_span(span_rows, tail, side, near, far):
    seqs, total, piece = near.shape
    width, extra = span_rows.shape[2], tail.shape[2]
    count = span_rows.shape[1] // (2 * piece)
    half = lambda s: (s, side, 0)
    table = pl.BlockSpec((1, total, piece), lambda s: (s, 0, 0))
    out = pl.BlockSpec((1, total, width + extra), lambda s: (s, 0, 0))
    return pl.pallas_call(
        functools.partial(pick_span_kernel, count, total // count),
        grid=(seqs,),
        in_specs=[
            pl.BlockSpec((1, count * piece, width), half),
            pl.BlockSpec((1, count * piece, extra), half),
            table,
            table,
        ],
        out_specs=[out] * 2,
        out_shape=[jax.ShapeDtypeStruct((seqs, total, width + extra), BF16)] * 2,
        cost_estimate=pl.CostEstimate(
            flops=4 * seqs * total * piece * width,
            transcendentals=0,
            bytes_accessed=2 * seqs * (count * piece + 2 * total) * width,
        ),
    )(span_rows, tail, near, far)


def place_kernel(counts, dest_ref, *refs):
    out = refs[-1]
    p = 0
    for ref, count in zip(refs, counts):
        rows = ref.shape[1] // count
        for q in range(count):
            start = pl.multiple_of(dest_ref[p] * rows, rows)
            out[0, pl.ds(start, rows), :] = ref[0, q * rows : (q + 1) * rows, :]
            p += 1


def place(arrays, dest, rows):
    seqs, _, width = arrays[0].shape
    counts = [array.shape[1] // rows for array in arrays]
    total = rows * sum(counts)
    first = lambda s, dest: (s, 0, 0)
    return pl.pallas_call(
        functools.partial(place_kernel, counts),
        grid_spec=pltpu.PrefetchScalarGridSpec(
            num_scalar_prefetch=1,
            grid=(seqs,),
            in_specs=[pl.BlockSpec((1, array.shape[1], width), first) for array in arrays],
            out_specs=pl.BlockSpec((1, total, width), first),
        ),
        out_shape=jax.ShapeDtypeStruct((seqs, total, width), BF16),
        cost_estimate=pl.CostEstimate(
            flops=0, transcendentals=0, bytes_accessed=4 * seqs * total * width
        ),
    )(dest, *arrays)


def project_kernel(count, transposed, rows_ref, weight_ref, *outs):
    dot = dot_nt if transposed else dot_nn
    result = dot(rows_ref[0], weight_ref[...]).astype(BF16)
    piece = outs[0].shape[1]
    for j in range(count):
        outs[j][0] = result[j * piece : (j + 1) * piece]


def project(span_rows, side, weight, count, transposed):
    seqs, total, depth = span_rows.shape
    group = total // 2
    width = weight.shape[0] if transposed else weight.shape[1]
    return pl.pallas_call(
        functools.partial(project_kernel, count, transposed),
        grid=(seqs,),
        in_specs=[
            pl.BlockSpec((1, group, depth), lambda s: (s, side, 0)),
            pl.BlockSpec(weight.shape, lambda s: (0, 0)),
        ],
        out_specs=[pl.BlockSpec((1, group // count, width), lambda s: (s, 0, 0))] * count,
        out_shape=[jax.ShapeDtypeStruct((seqs, group // count, width), BF16)] * count,
        cost_estimate=pl.CostEstimate(
            flops=2 * seqs * group * depth * width,
            transcendentals=0,
            bytes_accessed=2 * (seqs * group * (depth + width) + depth * width),
        ),
    )(span_rows, weight)


def spread_kernel(count, width, extra, *refs):
    base, near, near_rows, far, far_rows = refs[:5]
    outs = refs[6:] if extra else refs[5:]
    rows = outs[0].shape[1]
    slots = near.shape[1] // count
    for j in range(count):
        part = slice(j * slots, (j + 1) * slots)
        own = slice(j * rows, (j + 1) * rows)
        total = base[0, own, :].astype(F32)
        total = total + dot_tn(near[0, part, :], near_rows[0, part, :])
        total = total + dot_tn(far[0, part, :], far_rows[0, part, :])
        outs[j][0, :, :width] = total.astype(BF16)
        if extra:
            outs[j][0, :, width:] = refs[5][0, own, :]


def spread_blocks(base, side, near, near_rows, far, far_rows, columns=None):
    seqs, total, piece = near.shape
    width = base.shape[2]
    count = base.shape[1] // (2 * piece)
    group = count * piece
    first = lambda s: (s, 0, 0)
    table = pl.BlockSpec((1, total, piece), first)
    slot_rows = pl.BlockSpec((1, total, width), first)
    specs = [
        pl.BlockSpec((1, group, width), lambda s: (s, side, 0)),
        table,
        slot_rows,
        table,
        slot_rows,
    ]
    operands = [base, near, near_rows, far, far_rows]
    out_width = width
    if columns is not None:
        specs.append(pl.BlockSpec((1, group, columns.shape[2]), first))
        operands.append(columns)
        out_width = width + columns.shape[2]
    return pl.pallas_call(
        functools.partial(spread_kernel, count, width, columns is not None),
        grid=(seqs,),
        in_specs=specs,
        out_specs=[pl.BlockSpec((1, piece, out_width), first)] * count,
        out_shape=[jax.ShapeDtypeStruct((seqs, piece, out_width), BF16)] * count,
        cost_estimate=pl.CostEstimate(
            flops=4 * seqs * total * piece * width,
            transcendentals=0,
            bytes_accessed=4 * seqs * (group + total) * width,
        ),
    )(*operands)


def expert_kernel(
    top_count,
    mine_ref,
    tok_a,
    tok_b,
    raw_a,
    raw_b,
    router,
    gate_hbm,
    up_hbm,
    down_hbm,
    x_out,
    dy_out,
    hid_out,
    dgate_out,
    dup_out,
    dx_a,
    dx_b,
    out_a,
    out_b,
    dg_out,
    w_gate,
    w_up,
    w_down,
    gates,
    sems,
):
    half, width = tok_a.shape
    hidden = w_gate.shape[1]
    tile = 256
    spans = [(f, min(tile, hidden - f)) for f in range(0, hidden, tile)]

    def copies(i, start, size):
        cols = pl.ds(start, size)
        return (
            pltpu.make_async_copy(gate_hbm.at[0, :, cols], w_gate.at[:, cols], sems.at[0, i]),
            pltpu.make_async_copy(up_hbm.at[0, :, cols], w_up.at[:, cols], sems.at[1, i]),
            pltpu.make_async_copy(down_hbm.at[0, cols, :], w_down.at[cols, :], sems.at[2, i]),
        )

    for i, (start, size) in enumerate(spans):
        for copy in copies(i, start, size):
            copy.start()
    mine = mine_ref[0].astype(F32)
    for part, (tok, raw) in enumerate(((tok_a, raw_a), (tok_b, raw_b))):
        rows = slice(part * half, (part + 1) * half)
        x_out[rows, :] = tok[...]
        logits = dot_nt(tok[...], router[...])
        experts = lax.broadcasted_iota(jnp.int32, logits.shape, 1).astype(F32)
        named = raw[:, width:].astype(F32)
        routes = [named[:, j : j + 1] for j in range(top_count)]
        chosen = [
            jnp.sum(jnp.where(experts == r, logits, 0.0), axis=-1, keepdims=True) for r in routes
        ]
        best = functools.reduce(jnp.maximum, chosen)
        powers = [jnp.exp(c - best) for c in chosen]
        wanted = sum(jnp.where(r == mine, p, 0.0) for r, p in zip(routes, powers))
        gate = wanted / sum(powers)
        gates[rows, :] = gate
        dy_out[rows, :] = (raw[:, :width].astype(F32) * gate).astype(BF16)

    def hidden_part(i, start, size):
        for copy in copies(i, start, size):
            copy.wait()
        cols = pl.ds(start, size)
        gate = dot_nn(x_out[...], w_gate[:, cols])
        upward = dot_nn(x_out[...], w_up[:, cols])
        grad = dot_nt(dy_out[...], w_down[cols, :])
        sigmoid = 1.0 / (1.0 + jnp.exp(-gate))
        passed = gate * sigmoid
        hid_out[:, cols] = (passed * upward).astype(BF16)
        dgate_out[:, cols] = (
            grad * upward * sigmoid * (1.0 + gate * (1.0 - sigmoid))
        ).astype(BF16)
        dup_out[:, cols] = (grad * passed).astype(BF16)

    full = hidden // tile

    @pl.loop(0, full)
    def _(i):
        hidden_part(i, pl.multiple_of(i * tile, tile), tile)

    if full < len(spans):
        hidden_part(full, *spans[full])

    def width_part(n, dg):
        cols = pl.ds(pl.multiple_of(n * tile, tile), tile)
        result = dot_nn(hid_out[...], w_down[:, cols])
        grad = dot_nt(dgate_out[...], w_gate[cols, :]) + dot_nt(dup_out[...], w_up[cols, :])
        dx_a[:, cols] = grad[:half].astype(BF16)
        dx_b[:, cols] = grad[half:].astype(BF16)
        scaled = (result * gates[...]).astype(BF16)
        out_a[:, cols] = scaled[:half]
        out_b[:, cols] = scaled[half:]
        raw = jnp.concatenate([raw_a[:, cols], raw_b[:, cols]], axis=0).astype(F32)
        return dg + jnp.sum(raw * result, axis=-1, keepdims=True)

    dg_out[...] = lax.fori_loop(0, width // tile, width_part, jnp.zeros((2 * half, 1), F32))


def expert_rows(mine, tokens, grads, router, w_gate, w_up, w_down):
    half, width = tokens[0].shape
    hidden = w_gate.shape[2]
    rows = 2 * half
    parts = -(-hidden // 256)
    vmem = pl.BlockSpec(memory_space=pltpu.VMEM)
    shapes = [(rows, width)] * 2 + [(rows, hidden)] * 3 + [(half, width)] * 4
    return pl.pallas_call(
        functools.partial(expert_kernel, TOP),
        in_specs=[pl.BlockSpec(memory_space=pltpu.SMEM)]
        + [vmem] * 5
        + [pl.BlockSpec(memory_space=pl.ANY)] * 3,
        out_specs=[vmem] * 10,
        out_shape=[jax.ShapeDtypeStruct(shape, BF16) for shape in shapes]
        + [jax.ShapeDtypeStruct((rows, 1), F32)],
        scratch_shapes=[
            pltpu.VMEM((width, hidden), BF16),
            pltpu.VMEM((width, hidden), BF16),
            pltpu.VMEM((hidden, width), BF16),
            pltpu.VMEM((rows, 1), F32),
            pltpu.SemaphoreType.DMA((3, parts)),
        ],
        compiler_params=pltpu.CompilerParams(vmem_limit_bytes=60 * 1024 * 1024),
        cost_estimate=pl.CostEstimate(
            flops=12 * rows * width * hidden,
            transcendentals=rows * hidden,
            bytes_accessed=2 * (3 * width * hidden + 8 * rows * width + 3 * rows * hidden),
        ),
    )(mine, *tokens, *grads, router, w_gate, w_up, w_down)


def half_kernel(half_ref, far_in, near_in, *refs):
    count = 1
    fars, nears = refs[:count], refs[count : 2 * count]
    outs = refs[-count:]
    for j in range(count):
        total = dot_tn(far_in[...], fars[j][...]) + dot_tn(near_in[...], nears[j][...])
        if len(refs) > 3 * count:
            total = total + refs[2 * count + j][...].astype(F32)
        outs[j][...] = total.astype(outs[j].dtype)


def half_grads(far_in, near_in, far_grad, near_grad, half, received=None):
    depth, width = far_in.shape
    columns = far_grad.shape[1]
    tile = 512
    steps = width // 2 // tile
    taken = pl.BlockSpec((depth, tile), lambda i, half: (0, half[0] * steps + i))
    whole = pl.BlockSpec((depth, columns), lambda i, half: (0, 0))
    out = pl.BlockSpec((tile, columns), lambda i, half: (i, 0))
    operands = [far_in, near_in, far_grad, near_grad]
    specs = [taken] * 2 + [whole] * 2
    kind = BF16
    if received is not None:
        operands.append(received)
        specs.append(out)
        kind = F32
    return pl.pallas_call(
        half_kernel,
        grid_spec=pltpu.PrefetchScalarGridSpec(
            num_scalar_prefetch=1, grid=(steps,), in_specs=specs, out_specs=[out]
        ),
        out_shape=[jax.ShapeDtypeStruct((width // 2, columns), kind)],
        cost_estimate=pl.CostEstimate(
            flops=2 * depth * width * columns,
            transcendentals=0,
            bytes_accessed=2 * (depth * width + 2 * depth * columns + width * columns),
        ),
    )(half, *operands)[0]


def down_kernel(rank_ref, far_in, near_in, far_grad, near_grad, theirs, mine, total):
    half = theirs.shape[0]
    total[...] = dot_tn(far_in[...], far_grad[...]) + dot_tn(near_in[...], near_grad[...])
    rank = rank_ref[0]
    theirs[...] = total[pl.ds(pl.multiple_of((1 - rank) * half, 8), half), :].astype(BF16)
    mine[...] = total[pl.ds(pl.multiple_of(rank * half, 8), half), :].astype(BF16)


def down_grads(far_in, near_in, far_grad, near_grad, rank, side):
    depth, rows = far_in.shape
    width = far_grad.shape[1] // 2
    tile = 1024
    whole = pl.BlockSpec((depth, rows), lambda i, rank: (0, 0))
    piece = pl.BlockSpec((depth, tile), lambda i, rank: (0, side * (width // tile) + i))
    out = pl.BlockSpec((rows // 2, tile), lambda i, rank: (0, i))
    return pl.pallas_call(
        down_kernel,
        grid_spec=pltpu.PrefetchScalarGridSpec(
            num_scalar_prefetch=1,
            grid=(width // tile,),
            in_specs=[whole] * 2 + [piece] * 2,
            out_specs=[out] * 2,
            scratch_shapes=[pltpu.VMEM((rows, tile), F32)],
        ),
        out_shape=[jax.ShapeDtypeStruct((rows // 2, width), BF16)] * 2,
        cost_estimate=pl.CostEstimate(
            flops=4 * depth * rows * width,
            transcendentals=0,
            bytes_accessed=4 * depth * (rows + width) + 2 * rows * width,
        ),
    )(rank, far_in, near_in, far_grad, near_grad)


def merge_kernel(mine_a, mine_b, got_a, got_b, out):
    half = mine_a.shape[1]
    for j, (mine, got) in enumerate(((mine_a, got_a), (mine_b, got_b))):
        total = mine[...].astype(F32) + got[...].astype(F32)
        out[:, j * half : (j + 1) * half] = total


def merge_down(*parts):
    rows, half = parts[0].shape
    tile = rows // 4
    return pl.pallas_call(
        merge_kernel,
        grid=(4,),
        in_specs=[pl.BlockSpec((tile, half), lambda i: (i, 0))] * 4,
        out_specs=pl.BlockSpec((tile, 2 * half), lambda i: (i, 0)),
        out_shape=jax.ShapeDtypeStruct((rows, 2 * half), F32),
        cost_estimate=pl.CostEstimate(
            flops=0, transcendentals=0, bytes_accessed=16 * rows * half
        ),
    )(*parts)


def after(value, *others):
    return lax.optimization_barrier((value, *others))[0]


def layer(
    hidden_in,
    out_grad,
    routes,
    block_order,
    norm_attn,
    w_query,
    w_kv_down,
    norm_latent,
    w_key_up,
    w_value_up,
    w_out,
    norm_ffn,
    w_router,
    shared_gate,
    shared_up,
    shared_down,
    expert_gate,
    expert_up,
    expert_down,
):
    seqs, piece, width = hidden_in.shape
    n_expert = lax.axis_size(EXPERT)
    n_ctx = lax.axis_size(CTX)
    n_dp = lax.axis_size(DP)
    lanes = n_expert // 2
    heads = w_query.shape[1] // (NOPE + ROPE)
    expert_count = w_router.shape[1]
    slots = 8 * ((piece * TOP + 6 * expert_count - 1) // (6 * expert_count))
    expert_rank = lax.axis_index(EXPERT)
    ctx_rank = lax.axis_index(CTX)
    dp_rank = lax.axis_index(DP)
    span = piece * n_expert
    total_rows = span * n_ctx
    scale = (NOPE + ROPE) ** (-0.5)
    group = lanes * piece
    group_slots = lanes * slots

    def shift(value, steps):
        pairs = [(e, (e + 2 * steps) % n_expert) for e in range(n_expert)]
        return lax.ppermute(value, EXPERT, pairs)

    def across(value):
        return lax.ppermute(value, EXPERT, [(e, e ^ 1) for e in range(n_expert)])

    def other_dp(value):
        return lax.ppermute(value, DP, [(d, n_dp - 1 - d) for d in range(n_dp)])

    def other_ctx(value):
        return lax.ppermute(value, CTX, [(c, n_ctx - 1 - c) for c in range(n_ctx)])

    up_count = lanes // 2
    down_count = lanes - 1 - up_count

    def gather_blocks(own):
        ups, downs = [own], [own]
        for k in range(max(up_count, down_count)):
            if k < up_count:
                ups.append(shift(ups[-1], 1))
            if k < down_count:
                downs.append(shift(downs[-1], -1))
        column = ups + downs[:0:-1]
        return column + [across(b) for b in column]

    def gather_ctx(value):
        if n_ctx == 2:
            return [value, other_ctx(value)], [ctx_rank, 1 - ctx_rank]
        return [lax.all_gather(value, CTX, axis=1, tiled=True)], list(range(n_ctx))

    def scatter_ctx(value):
        if n_ctx == 2:
            half = value.shape[1] // 2
            return add(value[:, :half], other_ctx(value[:, half:]))
        return lax.psum_scatter(value, CTX, scatter_dimension=1, tiled=True)

    def add(*terms):
        total = terms[0].astype(F32)
        for term in terms[1:]:
            total = total + term.astype(F32)
        return total.astype(BF16)

    def scatter_blocks(part, hold=(), first=()):
        order = [up_count] + [k for k in range(lanes - 1, 0, -1) if k != up_count] + [0]
        crossed = {k: across(part(lanes + k)) for k in order}
        sums = {k: (part(k), crossed[k]) for k in order}
        marks = [crossed[up_count]]
        mine, got = sums[up_count]
        moving = add(after(mine, *first) if first else mine, got)
        for k in range(up_count, 0, -1):
            if k == 1 and hold:
                moving = after(moving, *hold)
            moving = shift(moving, -1)
            marks.append(moving)
            if k > 1:
                moving = add(*sums[k - 1], moving)
        result = [*sums[0], moving]
        if down_count:
            moving = add(*sums[lanes - down_count])
            for d in range(down_count, 0, -1):
                moving = shift(moving, 1)
                if d > 1:
                    moving = add(*sums[lanes - d + 1], moving)
            result.append(moving)
        return sum(term.astype(F32) for term in result), marks

    def sum_copies(grad, small=False):
        sent = grad.astype(BF16)
        if n_ctx != 2:
            return lax.psum(sent, (DP, CTX)).astype(F32)
        if small:
            pair = add(sent, other_ctx(sent))
            return pair.astype(F32) + other_dp(pair).astype(F32)
        half = grad.shape[0] // 2
        mine = lax.dynamic_slice_in_dim(sent, ctx_rank * half, half, 0)
        theirs = lax.dynamic_slice_in_dim(sent, (1 - ctx_rank) * half, half, 0)
        pair = add(mine, other_ctx(theirs))
        full = add(pair, other_dp(pair))
        rest = other_ctx(full)
        first = ctx_rank == 0
        return jnp.concatenate(
            [jnp.where(first, full, rest), jnp.where(first, rest, full)], axis=0
        ).astype(F32)

    def split_copies(grad):
        return lax.psum_scatter(
            grad.astype(BF16), CTX, scatter_dimension=0, tiled=True
        ).astype(F32)

    rank_z, rank_x = expert_rank // 2, expert_rank % 2
    owners = [
        ((rank_z - j % lanes) % lanes) * 2 + (rank_x + j // lanes) % 2 for j in range(n_expert)
    ]
    owner_ids = jnp.stack(owners)
    ids = jnp.arange(n_expert, dtype=jnp.int32)
    block_of = ((ids % 2 + rank_x) % 2) * lanes + (rank_z - ids // 2) % lanes

    tail = 2 * ROPE
    routes_tail = jnp.pad(routes.astype(BF16), ((0, 0), (0, 0), (0, tail - TOP)))
    blocks = gather_blocks(jnp.concatenate([hidden_in, routes_tail], axis=-1))

    kv_rows = w_kv_down.shape[0]
    kv_piece = kv_rows // n_ctx
    kv_own = lax.dynamic_slice_in_dim(w_kv_down, ctx_rank * kv_piece, kv_piece, 0)
    kv_blocks = gather_blocks(kv_own)
    kv_span = join([b[None] for b in kv_blocks])
    kv_all, ctx_ranks = gather_ctx(kv_span)
    ctx_ranks = jnp.stack([jnp.asarray(r, jnp.int32) for r in ctx_ranks])
    kv_dest = (owner_ids[None, :] * n_ctx + ctx_ranks[:, None]).reshape(-1)
    kv_full = place(kv_all, kv_dest, kv_piece)[0]

    def rms(rows):
        return lax.rsqrt(jnp.mean(rows * rows, axis=-1, keepdims=True) + EPSILON)

    half_rows = total_rows // (2 * n_ctx)

    def positions(row_ids):
        matches = (row_ids // half_rows)[:, None] == jnp.arange(2 * n_ctx, dtype=jnp.int32)
        starts = jnp.sum(jnp.where(matches[None], block_order[:, None, :], 0), axis=2)
        return starts * half_rows + row_ids % half_rows

    piece_ids = jnp.arange(piece, dtype=jnp.int32)
    in_span = (owner_ids[:, None] * piece + piece_ids[None, :]).reshape(-1)
    span_pos = positions(ctx_rank * span + in_span)
    key_pos = positions((ctx_ranks[:, None] * span + in_span[None, :]).reshape(-1))
    tables = rope_tables(span_pos)
    span_cos, span_sin = tables
    turns = jnp.concatenate([span_cos, span_cos, span_sin, span_sin], axis=-1)
    span_cos = jnp.tile(span_cos, (1, 1, 2 * heads))
    span_sin = jnp.tile(span_sin, (1, 1, 2 * heads))

    per_head = w_query.reshape(width, heads, NOPE + ROPE)
    w_nope = per_head[..., :NOPE].reshape(width, heads * NOPE)
    w_rope = per_head[..., NOPE:]
    first, second = halves(w_rope)
    w_turned = jnp.concatenate([-second, first], axis=-1).reshape(width, heads * ROPE)
    w_inner = jnp.concatenate([w_nope, w_rope.reshape(width, heads * ROPE), w_turned], axis=-1)
    w_up = jnp.concatenate([w_key_up, w_value_up], axis=-1)
    shared_width = shared_gate.shape[1]
    shared_room = -(-shared_width // 128) * 128
    spare = ((0, shared_room - shared_width), (0, 0))
    w_shared = jnp.concatenate([jnp.pad(shared_gate.T, spare), jnp.pad(shared_up.T, spare)], axis=0)
    w_shared_down = jnp.pad(shared_down, spare)
    w_inner, w_up, w_shared, w_shared_down = lax.optimization_barrier(
        (w_inner, w_up, w_shared, w_shared_down)
    )

    own_rows = hidden_in.astype(F32)
    inv_own = rms(own_rows)
    normed_span, routes_cols = join_norm(
        [
            after(blocks[0], span_cos, span_sin, turns, w_inner, w_shared, w_shared_down),
            *blocks[1:],
        ], norm_attn
    )
    grad_all = lax.all_gather(after(out_grad, normed_span), EXPERT, axis=1, tiled=True)
    kv_joint = product(normed_span, kv_full)
    latent_raw = kv_joint[..., :LATENT]
    inv_latent = rms(latent_raw)
    key_rope = rotate(kv_joint[..., LATENT:], tables)
    rope_first, rope_second = halves(key_rope)
    latent_span = jnp.concatenate(
        [latent_raw * inv_latent * norm_latent, key_rope, rope_second, -rope_first], axis=-1
    ).astype(BF16)
    latent_all = gather_ctx(latent_span)[0]
    latent_all = jnp.concatenate(latent_all, axis=1) if len(latent_all) > 1 else latent_all[0]
    query_raw = product(normed_span, w_inner)
    flat = heads * NOPE
    queries = jnp.concatenate(
        [
            query_raw[..., :flat],
            query_raw[..., flat : flat + heads * ROPE] * span_cos
            + query_raw[..., flat + heads * ROPE :] * span_sin,
        ],
        axis=-1,
    ).astype(BF16)
    latent_part = latent_all[..., :LATENT]
    pairs = product(latent_part, w_up).astype(BF16)
    heads_out, lse = attend(queries, pairs, latent_all, span_pos, key_pos, heads, scale)

    def block_of_span(array, j):
        return array[:, j * piece : (j + 1) * piece]

    routes_span = routes_cols[..., :TOP].astype(jnp.int32).reshape(seqs, n_expert, piece, TOP)
    mine = dp_rank * n_expert + expert_rank
    theirs = (n_dp - 1 - dp_rank) * n_expert + expert_rank
    earlier = (piece_ids[:, None] < piece_ids[None, :]).astype(F32)
    slot_ids = jnp.arange(slots, dtype=jnp.int32)
    picks = []
    for target in (mine, theirs):
        named = jnp.any(routes_span == target, axis=-1)
        rank = jnp.einsum("sjp,pq->sjq", named.astype(F32), earlier).astype(jnp.int32)
        picks.append(jnp.where(named, rank, -1)[:, :, None, :] == slot_ids[:, None])

    def side_tables(table):
        return [
            table[:, side * lanes : (side + 1) * lanes].reshape(seqs, group_slots, piece)
            for side in range(2)
        ]

    near_tables = side_tables(picks[0].astype(BF16))
    far_tables = side_tables(picks[1].astype(BF16))
    grad_span = place([grad_all], block_of, piece)
    grad_slots = [
        pick_span(grad_span, routes_cols, side, near_tables[side], far_tables[side])
        for side in range(2)
    ]
    grad_got = [other_dp(grad_slots[side][1]) for side in range(2)]
    sh_dhidden = back_product(grad_span, w_shared_down)

    def project_sides(rows, weight, transposed):
        far_side = project(rows, 1, weight, lanes, transposed)
        near_side = project(rows, 0, weight, lanes, transposed)
        return lambda j: (near_side, far_side)[j // lanes][j % lanes]

    attn_own, _ = scatter_blocks(
        project_sides(heads_out, w_out, False),
        hold=(sh_dhidden, grad_slots[0][1], grad_slots[1][1]),
    )
    residual = own_rows + attn_own
    inv_ffn = rms(residual)
    unit_ffn = residual * inv_ffn
    normed_ffn = (unit_ffn * norm_ffn).astype(BF16)
    ffn_blocks = gather_blocks(normed_ffn)
    token_slots = [
        pick_blocks(
            ffn_blocks[side * lanes : (side + 1) * lanes], near_tables[side], far_tables[side]
        )
        for side in range(2)
    ]
    token_got = [other_dp(token_slots[side][1]) for side in range(2)]
    ffn_span = join([after(b, token_slots[1][1]) for b in ffn_blocks])

    sh_both = back_product(ffn_span, w_shared)
    sh_gate, sh_up = sh_both[..., :shared_room], sh_both[..., shared_room:]
    sh_hidden = (jax.nn.silu(sh_gate) * sh_up).astype(BF16)
    sh_dboth = jnp.concatenate(silu_grads(sh_dhidden, sh_gate, sh_up), axis=-1)
    sh_dnorm = product(sh_dboth, w_shared).astype(BF16)

    slot_shape = (seqs, group_slots)

    def expert(tokens, grads):
        rows = [t.reshape(seqs * group_slots, -1) for t in (*tokens, *grads)]
        results = expert_rows(
            mine.reshape(1),
            rows[:2],
            rows[2:],
            w_router.T,
            expert_gate,
            expert_up,
            expert_down,
        )
        dx, out = [
            [side.reshape(*slot_shape, width) for side in pair]
            for pair in (results[5:7], results[7:9])
        ]
        return results[:5], dx, out, results[9].reshape(2, *slot_shape)

    far, far_dx, far_out, far_dg = expert([after(t, sh_dnorm) for t in token_got], grad_got)
    dg_back = other_dp(far_dg)
    dx_back = [None, None]
    dx_back[1] = other_dp(far_dx[1])
    dx_back[0] = other_dp(far_dx[0])
    out_back = [other_dp(after(far_out[side], *dx_back)) for side in range(2)]
    near, near_dx, near_out, near_dg = expert(
        [after(t[0], far_dx[1]) for t in token_slots], [g[0] for g in grad_slots]
    )

    lane_ids = jnp.arange(128, dtype=jnp.int32)

    def dg_columns(side):
        columns = 0.0
        for pick, dg, target in ((picks[0], near_dg, mine), (picks[1], dg_back, theirs)):
            table = pick[:, side * lanes : (side + 1) * lanes]
            values = dg[side].reshape(seqs, lanes, slots, 1)
            rows = jnp.sum(jnp.where(table, values, 0.0), axis=2).reshape(seqs, group, 1)
            top = rows.astype(BF16).astype(F32)
            columns = columns + jnp.where(lane_ids == target, top, 0.0)
            columns = columns + jnp.where(lane_ids == target + expert_count, rows - top, 0.0)
        return columns.astype(BF16)

    dnorm_blocks = []
    for side in range(2):
        dnorm_blocks.append(
            spread_blocks(
                sh_dnorm,
                side,
                near_tables[side],
                near_dx[side],
                far_tables[side],
                dx_back[side],
                dg_columns(side),
            )
        )
    dnorm_sum, marks = scatter_blocks(lambda j: dnorm_blocks[j // lanes][j % lanes])

    grad_sh_in = weight_grad(sh_dboth, ffn_span).astype(BF16)
    grad_sh_down = weight_grad(sh_hidden, grad_span).astype(BF16)
    grad_sh_in, grad_sh_down = lax.psum(
        (after(grad_sh_in, dnorm_blocks[0][0]), after(grad_sh_down, dnorm_blocks[0][0])),
        (DP, CTX),
    )

    dg_own = (
        dnorm_sum[..., width : width + expert_count]
        + dnorm_sum[..., width + expert_count : width + 2 * expert_count]
    )
    dnorm_sum = dnorm_sum[..., :width]
    route_hot = routes[..., None] == jnp.arange(expert_count, dtype=jnp.int32)
    logits = product(normed_ffn, w_router)
    chosen = jnp.sum(jnp.where(route_hot, logits[:, :, None, :], 0.0), axis=-1)
    gate_weights = jax.nn.softmax(chosen, axis=-1)
    grad_choice = jnp.sum(jnp.where(route_hot, dg_own[:, :, None, :], 0.0), axis=-1)
    grad_chosen = gate_weights * (
        grad_choice - jnp.sum(gate_weights * grad_choice, axis=-1, keepdims=True)
    )
    grad_logits = jnp.sum(jnp.where(route_hot, grad_chosen[..., None], 0.0), axis=2).astype(BF16)
    dnorm_ffn = dnorm_sum + back_product(grad_logits, w_router)
    grad_resid = out_grad.astype(F32) + norm_back(dnorm_ffn, residual, inv_ffn, norm_ffn)
    attn_blocks = gather_blocks(grad_resid.astype(BF16))
    grad_attn = join(attn_blocks)
    grad_router = weight_grad(normed_ffn, after(grad_logits, attn_blocks[1]))
    grad_gain_ffn = jnp.sum(after(dnorm_ffn, attn_blocks[1]) * unit_ffn, axis=(0, 1))

    sh_out = product(after(sh_hidden, marks[1]), w_shared_down).astype(BF16)
    out_blocks = []
    for side in range(2):
        out_blocks += spread_blocks(
            sh_out,
            side,
            near_tables[side],
            near_out[side],
            far_tables[side],
            out_back[side],
        )
    out_part = place(out_blocks, owner_ids, piece)
    out_own = lax.psum_scatter(out_part, EXPERT, scatter_dimension=1, tiled=True)
    out_hidden = (residual + out_own.astype(F32)).astype(BF16)

    if n_ctx == 2:
        rank = ctx_rank.reshape(1)
        ready = after(rank, dnorm_blocks[0][0])
        got = []
        for i in (3, 4):
            part = half_grads(far[0], near[0], far[i], near[i], 1 - ready)
            got.append(other_ctx(part))
        down_mine = []
        for side in range(2):
            part, own = down_grads(far[2], near[2], far[1], near[1], ready, side)
            got.append(other_ctx(part))
            down_mine.append(own)
    else:
        rows_in, grads_in, ex_hidden, ex_dgate, ex_dup = [
            jnp.concatenate([f, n], axis=0) for f, n in zip(far[:5], near[:5])
        ]
        exp_grads = [
            split_copies(weight_grad(rows_in, ex_dgate)),
            split_copies(weight_grad(rows_in, ex_dup)),
            split_copies(weight_grad(ex_hidden, grads_in)),
        ]

    grad_heads = back_product(grad_attn, w_out).astype(BF16)
    grad_queries, grad_pairs, grad_key_rope = attend_back(
        queries, pairs, latent_all, grad_heads, lse, span_pos, key_pos, turns, heads, scale
    )
    grad_latent = jnp.concatenate(
        [back_product(grad_pairs, w_up).astype(BF16), grad_key_rope], axis=-1
    )

    def by_rank(array):
        return array.reshape(n_expert, -1)

    def padded(array, size):
        return jnp.pad(array, ((0, 0), (0, size - array.shape[1])))

    room = seqs * piece * ROPE
    early = jnp.concatenate([by_rank(grad_gain_ffn), by_rank(grad_router)], axis=1)
    early_size = early.shape[1]
    early = jnp.take(padded(early, room).astype(BF16), owner_ids, axis=0, mode="clip")
    early = early.reshape(n_expert, seqs, piece, ROPE).transpose(1, 0, 2, 3)
    grad_latent_span = jnp.concatenate(
        [scatter_ctx(grad_latent), early.reshape(seqs, span, ROPE)], axis=-1
    )
    dnorm_own, marks = scatter_blocks(
        project_sides(grad_queries, w_query, True), first=(grad_latent_span,)
    )
    grad_latent_own, lat_marks = scatter_blocks(lambda j: block_of_span(grad_latent_span, j))
    early = grad_latent_own[..., LATENT + ROPE :].reshape(-1)[:early_size]

    grad_query_part = weight_grad(normed_span, after(grad_queries, lat_marks[1]))
    grad_up_part = weight_grad(latent_part, after(grad_pairs, lat_marks[1]))
    grad_out_part = weight_grad(heads_out, grad_attn)
    grad_query_w = sum_copies(grad_query_part)
    grad_out_w = sum_copies(grad_out_part)
    grad_up = sum_copies(grad_up_part, small=True)
    if n_ctx == 2:
        exp_grads = []
        for i in range(2):
            exp_grads.append(
                half_grads(far[0], near[0], far[3 + i], near[3 + i], rank, got[i])
            )
    gain_part = jnp.sum(grad_query_part * w_query.astype(F32), axis=-1) / norm_attn
    gain_latent_part = jnp.sum(grad_up_part * w_up.astype(F32), axis=-1) / norm_latent
    late = jnp.concatenate([by_rank(gain_part), by_rank(gain_latent_part)], axis=1)
    late_size = late.shape[1]
    late = padded(late.reshape(1, -1), room).astype(BF16).reshape(seqs, piece, ROPE)

    grad_unit = grad_latent_own[..., :LATENT]
    own_tables = [table[:, :piece] for table in tables]
    grad_kv = jnp.concatenate(
        [
            norm_back(grad_unit, latent_raw[:, :piece], inv_latent[:, :piece], norm_latent),
            unrotate(grad_latent_own[..., LATENT : LATENT + ROPE], own_tables),
        ],
        axis=-1,
    ).astype(BF16)
    kv_grads = gather_blocks(jnp.concatenate([grad_kv, late], axis=-1))
    grad_kv_span = join(kv_grads)
    shared_sums = lax.optimization_barrier(
        (grad_sh_in, grad_sh_down, kv_grads[lanes])
    )[:2]
    shared_grads = [
        shared_sums[0][:shared_width].astype(F32).T,
        shared_sums[0][shared_room : shared_room + shared_width].astype(F32).T,
        shared_sums[1][:shared_width].astype(F32),
    ]
    if n_ctx == 2:
        exp_grads.append(merge_down(*down_mine, *got[2:]))
    normed_cols = lax.dynamic_slice_in_dim(normed_span, expert_rank * kv_rows, kv_rows, 2)
    late = (
        grad_kv_span[..., LATENT + ROPE :]
        .reshape(seqs, n_expert, piece, ROPE)
        .transpose(1, 0, 2, 3)
        .reshape(n_expert, -1)[:, : n_expert * late_size]
        .reshape(n_expert, n_expert, late_size)
    )
    late = jnp.sum(
        lax.dynamic_index_in_dim(late, expert_rank, 1, False).astype(F32), axis=0
    )
    rows = width // n_expert
    small = padded(jnp.concatenate([late, early])[None], kv_rows * ROPE).reshape(kv_rows, ROPE)
    kv_part = jnp.concatenate(
        [weight_grad(normed_cols, grad_kv_span[..., : LATENT + ROPE]), small], axis=-1
    ).astype(BF16)
    if n_ctx == 2:
        kv_pair = add(kv_part, other_ctx(kv_part))
        kv_small = kv_pair.astype(F32) + other_dp(kv_pair).astype(F32)
    else:
        kv_pair = kv_part
        kv_small = lax.psum(kv_part, (DP, CTX)).astype(F32)
    dnorm_kv = back_product(after(grad_kv, kv_pair), kv_full)
    in_grad = (
        grad_resid + norm_back(dnorm_own + dnorm_kv, own_rows, inv_own, norm_attn)
    ).astype(BF16)
    grad_kv_w = kv_small[:, : LATENT + ROPE]
    small = kv_small[:, LATENT + ROPE :].reshape(-1)
    late, early = small[:late_size], small[late_size : late_size + early_size]
    own_gain = lax.dynamic_slice_in_dim(norm_attn, expert_rank * rows, rows, 0)
    gain_kv = jnp.sum(grad_kv_w * w_kv_down.astype(F32), axis=-1) / own_gain
    return (
        out_hidden,
        in_grad,
        late[:rows] + gain_kv,
        grad_query_w,
        grad_kv_w,
        late[rows:],
        grad_up[:, :flat],
        grad_up[:, flat:],
        grad_out_w,
        early[:rows],
        early[rows:].reshape(rows, expert_count),
        *shared_grads,
        exp_grads[0][None],
        exp_grads[1][None],
        exp_grads[2][None],
    )


def solution(mesh):
    return jax.shard_map(
        layer,
        mesh=mesh,
        in_specs=(
            P(DP, (CTX, EXPERT), None),
            P(DP, (CTX, EXPERT), None),
            P(DP, (CTX, EXPERT), None),
            P(DP, None),
            P(),
            P(None, EXPERT),
            P(EXPERT, None),
            P(),
            P(None, EXPERT),
            P(None, EXPERT),
            P(EXPERT, None),
            P(),
            P(),
            P(None, EXPERT),
            P(None, EXPERT),
            P(EXPERT, None),
            P((DP, EXPERT), None, None),
            P((DP, EXPERT), None, None),
            P((DP, EXPERT), None, None),
        ),
        out_specs=(
            P(DP, (CTX, EXPERT), None),
            P(DP, (CTX, EXPERT), None),
            P(EXPERT),
            P(None, EXPERT),
            P(EXPERT, None),
            P(EXPERT),
            P(None, EXPERT),
            P(None, EXPERT),
            P(EXPERT, None),
            P(EXPERT),
            P(EXPERT, None),
            P(None, EXPERT),
            P(None, EXPERT),
            P(EXPERT, None),
            P((DP, EXPERT), CTX, None),
            P((DP, EXPERT), CTX, None),
            P((DP, EXPERT), CTX, None),
        ),
        check_vma=False,
    )
```
